32 devices in a mesh: grp: 2 (over x), chan: 16 (over z, y, core).
Axes of the slice: x: 2, y: 2, z: 4, core: 2. Of those that a mesh axis runs over, the one named last changes fastest.
Arguments:
- spectra: bfloat16 [2048, 2, 64, 512], P(('grp', 'chan')), parts along dimension 0, may hold values from -6 to 6
- valid: int32 [2048, 64], P(('grp', 'chan')), parts along dimension 0, may hold values 0 or 1
- sources: int32 [32], P('grp'), parts along dimension 0, may hold values from 0 to 1023
Outputs:
- smoothed: float32 [32, 1024, 1024], P('grp', 'chan'), parts along dimension 0
The draws below stay inside these ranges and needn't reach their ends.
There are 2 independent parts, one for each index of `grp`. The reference program is written for one: setup_inputs(seed, part) draws one part's arguments, and reference() takes and returns one part's arrays. A program takes and returns all parts, laid end to end along the dimension named above; each array names one. Nothing has to cross between parts.
Inputs may be any that keep to these rules, and one draw needn't show every extreme that they name: `sources`: channel indices of the segment; repeats may occur.
All inputs are finite; a program needn't handle non-finite values. No bound on the sum of `valid` on one device may be relied on, other than what follows from the above.
Results may differ from the reference program's by a relative error of at most 0.0037.
Values may be sent and summed in bfloat16 or wider, within the bound.
A program may use at most 128 MiB of HBM per device.

```python
import jax
import jax.numpy as jnp
from jax import lax

F = 512
S = 16
W = 64
CH_DEV = 64
CHANNELS = 1024
NL = 1024


def place_ends(drawn, rng, low, high):
    shape = drawn.shape
    place = [jax.random.randint(jax.random.fold_in(rng, axis), (), 0, shape[axis]) for axis in range(len(shape))]
    drawn = drawn.at[tuple(place)].set(low)
    longest = shape.index(max(shape))
    place[longest] = (place[longest] + 1) % shape[longest]
    return drawn.at[tuple(place)].set(high)


def levels(rng, extent, cuts, smallest, largest):
    factor_of = 1.0
    for axis_at, shards_of in cuts:
        draws = jax.random.uniform(jax.random.fold_in(jax.random.fold_in(rng, 6), axis_at), (shards_of,), jnp.float32, smallest / len(cuts), largest / len(cuts))
        factor_of = factor_of * jnp.repeat(jnp.exp(draws), extent[axis_at] // shards_of).reshape((-1,) + (1,) * (len(extent) - 1 - axis_at))
    return factor_of


def centred(stream_key, extent, width, limit, shards=(), kind=jnp.bfloat16):
    array = jax.random.normal(stream_key, extent, jnp.float32) * width
    if len(shards) > 0:
        array = levels(stream_key, extent, shards, -0.22, 0.18) * array
    return jnp.clip(array, min=-limit, max=limit).astype(kind)


def setup_inputs(seed: int = 0, part: int = 0) -> dict:
    splits = jax.random.split(jax.random.key(seed), 4)
    part_splits = jax.random.split(jax.random.fold_in(splits[3], part), 4)
    return {
        "spectra": centred(part_splits[0], (CHANNELS, 2, W, F), 1.0, 6.0, ((0, 16),)),
        "valid": place_ends((jax.random.randint(part_splits[1], (CHANNELS, W), 0, 4) < 3).astype(jnp.int32), jax.random.fold_in(part_splits[1], 1), 0, 1),
        "sources": place_ends(jax.random.randint(part_splits[2], (S,), 0, CHANNELS), jax.random.fold_in(part_splits[2], 1), 0, CHANNELS - 1).astype(jnp.int32),
    }


def make_table(nbins, nlags):
    freq = jnp.arange(nbins, dtype=jnp.int32)
    lagidx = jnp.arange(nlags, dtype=jnp.int32)
    phase = ((freq[:, None] * lagidx[None, :]) % nlags).astype(jnp.float32)
    angle = 2.0 * jnp.pi * phase / nlags
    weight = jnp.where(freq == 0, 1.0, 2.0).astype(jnp.float32) / nlags
    cosine = weight[:, None] * jnp.cos(angle)
    sine = -weight[:, None] * jnp.sin(angle)
    return jnp.concatenate([cosine, sine], axis=0).astype(jnp.bfloat16)


def reference(spectra, valid, sources):
    src_spec = spectra[sources].astype(jnp.float32)
    src_valid = valid[sources].astype(jnp.float32)
    src_m = src_spec * src_valid[:, None, :, None]
    table = make_table(F, NL)
    blocks = CHANNELS // CH_DEV
    spec_blocks = spectra.reshape(blocks, CH_DEV, 2, W, F)
    valid_blocks = valid.reshape(blocks, CH_DEV, W)

    def one_block(pair):
        spec_b, valid_b = pair
        chan_m = spec_b.astype(jnp.float32) * valid_b.astype(jnp.float32)[:, None, :, None]
        aa = jnp.einsum('swf,cwf->scf', src_m[:, 0], chan_m[:, 0])
        bb = jnp.einsum('swf,cwf->scf', src_m[:, 1], chan_m[:, 1])
        ad = jnp.einsum('swf,cwf->scf', src_m[:, 0], chan_m[:, 1])
        bc = jnp.einsum('swf,cwf->scf', src_m[:, 1], chan_m[:, 0])
        cross = jnp.concatenate([(aa + bb) / W, (ad - bc) / W], axis=2).astype(jnp.bfloat16)
        flat = cross.reshape(S * CH_DEV, 2 * F)
        return jnp.dot(flat, table, preferred_element_type=jnp.float32).reshape(S, CH_DEV, NL)

    lag_blocks = lax.map(one_block, (spec_blocks, valid_blocks))
    lags = jnp.transpose(lag_blocks, (1, 0, 2, 3)).reshape(S, CHANNELS, NL)
    padded = jnp.pad(lags, ((0, 0), (2, 2), (0, 0)))
    total = padded[:, 0:CHANNELS] + padded[:, 1:CHANNELS + 1] + padded[:, 2:CHANNELS + 2]
    total = total + padded[:, 3:CHANNELS + 3] + padded[:, 4:CHANNELS + 4]
    return total / 5.0
```

```python
import functools

import jax
import jax.numpy as jnp
import numpy as np
from jax import lax
from jax.experimental import pallas as pl
from jax.experimental.pallas import tpu as pltpu
from jax.sharding import PartitionSpec as P

MESH = pl.DeviceIdType.MESH
HALO = 2
LAG = 4
ENTER = 2
SETTLE = 2
LOADED = 4
FB = 128
ACROSS, BACK, IN_UP, IN_DOWN, ON_UP, ON_DOWN, OUT_UP, OUT_DOWN = range(8)
KINDS = 8


def make_table(nbins, nlags):
    freq = np.arange(nbins, dtype=np.int64)
    phase = (freq[:, None] * np.arange(nlags, dtype=np.int64)[None, :]) % nlags
    angle = 2.0 * np.pi * phase / nlags
    weight = np.where(freq == 0, 1.0, 2.0) / nlags
    table = np.concatenate([weight[:, None] * np.cos(angle), -weight[:, None] * np.sin(angle)])
    return table.astype(np.float32).astype(jnp.bfloat16)


def cross_kernel(outer, inner, nrow, src_ref, valid_ref, spec_ref, flat_ref,
                 first, spec, halo, halo_valid, flags, plane, give, own, part, inward, along, passed, gathered,
                 chan_t, src_t, cross_t, load_sem, send_sem, recv_sem, edge_send, edge_recv):
    nblk, nchan, depth, _ = spec.shape
    nsrc, nwin, _ = plane.shape
    per = nsrc // 2
    n = nblk * per
    size = outer * inner * 2
    me = lax.axis_index("chan")
    core, chip = me % 2, me // 2
    j, i = chip % inner, chip // inner
    line_j, line_i = (j, inner, 2), (i, outer, 2 * inner)
    teeth, spine = (line_j, line_i), (line_i, line_j)
    partner = me + 1 - 2 * core
    pitch, cpitch = FB + 1, 2 * nsrc + 1

    def reach(q):
        length = teeth[q][1]
        return length - 1 if q == 0 else length - 1 - (length - 1) // 2

    def root(q, k):
        length = teeth[q][1]
        if length == 1:
            return 0
        return k % length if q == 0 else (length - 1) // 2 + k % 2

    rooted = [ENTER + LAG * reach(q) for q in range(2)]
    summed = [rooted[q] + LAG * (spine[q][1] - 1) for q in range(2)]
    settled = max(summed[q] + LAG * reach(q) for q in range(2)) + SETTLE
    turn_at = settled - per

    def load(b):
        return pltpu.make_async_copy(spec_ref.at[:, :, pl.ds(b * FB, FB)], spec.at[b], load_sem.at[1 + b])

    load_first = pltpu.make_async_copy(spec_ref.at[:, :, pl.ds(0, FB)], first, load_sem.at[0])
    load_first.start()
    for b in range(nblk):
        load(b).start()

    barrier = pltpu.get_barrier_semaphore()

    def greet(there):
        pl.semaphore_signal(barrier, inc=1, device_id={"chan": there}, device_id_type=MESH)

    greet(partner)
    count = jnp.int32(1)
    for pos, length, stride in (line_j, line_i, (me, size, 1)):
        @pl.when(pos > 0)
        def _():
            greet(me - stride)

        @pl.when(pos < length - 1)
        def _():
            greet(me + stride)

        count = count + (pos > 0).astype(jnp.int32) + (pos < length - 1).astype(jnp.int32)

    raw = valid_ref[...].astype(jnp.float32)
    flags[...] = jnp.concatenate([raw, raw], axis=1)
    by_window = jnp.transpose(flags[...])[0:nwin].astype(jnp.bfloat16)
    place = lax.broadcasted_iota(jnp.int32, (nchan, FB), 0)
    for s in range(nsrc):
        hot = (place == src_ref[s] - me * nchan).astype(jnp.bfloat16)
        plane[s] = jnp.dot(by_window, hot, preferred_element_type=jnp.float32).astype(jnp.bfloat16)

    pl.semaphore_wait(barrier, count)

    def edges(up):
        there = me + 1 if up else me - 1
        side, rows = (0, nchan - HALO) if up else (1, 0)
        eight = nchan - 8 if up else 0
        return [pltpu.make_async_remote_copy(
                    src_ref=spec_ref.at[pl.ds(rows, HALO)], dst_ref=halo.at[pl.ds(side * HALO, HALO)],
                    send_sem=edge_send.at[side, 0], recv_sem=edge_recv.at[side, 0],
                    device_id={"chan": there}, device_id_type=MESH),
                pltpu.make_async_remote_copy(
                    src_ref=valid_ref.at[pl.ds(eight, 8)], dst_ref=halo_valid.at[side],
                    send_sem=edge_send.at[side, 1], recv_sem=edge_recv.at[side, 1],
                    device_id={"chan": there}, device_id_type=MESH)]

    @pl.when(me < size - 1)
    def _():
        for copy in edges(True):
            copy.start()

    @pl.when(me > 0)
    def _():
        for copy in edges(False):
            copy.start()

    def remote(src, dst, kind, q, k, there):
        return pltpu.make_async_remote_copy(
            src_ref=src, dst_ref=dst, send_sem=send_sem.at[kind, q, k], recv_sem=recv_sem.at[kind, q, k],
            device_id={"chan": there}, device_id_type=MESH)

    def spot(q, k, half):
        return (2 * k + q) * 2 + half

    def across(q, k):
        return remote(give.at[q, k], part.at[q, k], ACROSS, q, k, partner)

    def back(q, k, half):
        at = spot(q, k, half)
        return remote(gathered.at[at], gathered.at[at], BACK, q, k, partner)

    def toward(q, up, k):
        there = me + teeth[q][2] if up else me - teeth[q][2]
        return remote(own.at[q, k], inward.at[0 if up else 1, q, k], IN_UP if up else IN_DOWN, q, k, there)

    def onward(q, up, k, src):
        there = me + spine[q][2] if up else me - spine[q][2]
        return remote(src, along.at[0 if up else 1, q, k], ON_UP if up else ON_DOWN, q, k, there)

    def outward(q, up, k):
        there = me + teeth[q][2] if up else me - teeth[q][2]
        at = spot(q, k, core)
        return remote(gathered.at[at], gathered.at[at], OUT_UP if up else OUT_DOWN, q, k, there)

    def prepare(block, s, q, k):
        held = jnp.clip(src_ref[s] - me * nchan, 0, nchan - 1)
        mask = plane[s]
        give[q, k] = block[held, pl.ds((1 - core) * nwin, nwin)] * mask
        own[q, k] = block[held, pl.ds(core * nwin, nwin)] * mask
        across(q, k).start()

    def guarded(k, also, run):
        @pl.when((k >= 0) & (k < n) & also)
        def _():
            run(k)

    def enter(q, k):
        pos, length, _ = teeth[q]
        across(q, k).wait_recv()
        own[q, k] = own[q, k] + part[q, k]
        if length > 1:
            @pl.when((pos == 0) & (root(q, k) > 0))
            def _():
                toward(q, True, k).start()

            @pl.when((pos == length - 1) & (root(q, k) < length - 1))
            def _():
                toward(q, False, k).start()

    def relay_in(q, t):
        pos, length, _ = teeth[q]
        if length <= 2:
            return

        def run(up):
            def go(k):
                @pl.when(pos < root(q, k) if up else pos > root(q, k))
                def _():
                    toward(q, up, k).wait_recv()
                    own[q, k] = own[q, k] + inward[0 if up else 1, q, k]
                    toward(q, up, k).start()

            steps = pos if up else length - 1 - pos
            guarded(t - LAG * steps, steps > 0, go)

        run(True)
        run(False)

    def reach_root(q, k):
        pos, length, _ = teeth[q]
        at, span, _ = spine[q]

        @pl.when(pos == root(q, k))
        def _():
            if length > 1:
                @pl.when(pos > 0)
                def _():
                    toward(q, True, k).wait_recv()
                    own[q, k] = own[q, k] + inward[0, q, k]

                @pl.when(pos < length - 1)
                def _():
                    toward(q, False, k).wait_recv()
                    own[q, k] = own[q, k] + inward[1, q, k]
            if span > 1:
                @pl.when(at == 0)
                def _():
                    onward(q, True, k, own.at[q, k]).start()

                @pl.when(at == span - 1)
                def _():
                    onward(q, False, k, own.at[q, k]).start()

    def relay_on(q, t):
        pos, length, _ = teeth[q]
        at, span, _ = spine[q]
        if span == 1:
            return

        def run(up):
            def go(k):
                @pl.when(pos == root(q, k))
                def _():
                    onward(q, up, k, own.at[q, k]).wait_recv()
                    if span > 2:
                        @pl.when(at < span - 1 if up else at > 0)
                        def _():
                            passed[0 if up else 1, q, k] = own[q, k] + along[0 if up else 1, q, k]
                            onward(q, up, k, passed.at[0 if up else 1, q, k]).start()

            steps = at if up else span - 1 - at
            guarded(t - LAG * steps, steps > 0, go)

        run(True)
        run(False)

    def finish(q, k):
        pos, length, _ = teeth[q]
        at, span, _ = spine[q]

        @pl.when(pos == root(q, k))
        def _():
            to = spot(q, k, core)
            if span == 1:
                gathered[to] = own[q, k]
            else:
                @pl.when(at == 0)
                def _():
                    gathered[to] = own[q, k] + along[1, q, k]

                @pl.when(at == span - 1)
                def _():
                    gathered[to] = own[q, k] + along[0, q, k]

                if span > 2:
                    @pl.when((at > 0) & (at < span - 1))
                    def _():
                        gathered[to] = own[q, k] + along[0, q, k] + along[1, q, k]
            if length > 1:
                @pl.when(pos < length - 1)
                def _():
                    outward(q, True, k).start()

                @pl.when(pos > 0)
                def _():
                    outward(q, False, k).start()
            back(q, k, core).start()

    def spread(q, t):
        pos, length, _ = teeth[q]
        if length == 1:
            return

        def run(far, up):
            def go(k):
                @pl.when(pos - root(q, k) == (far if up else -far))
                def _():
                    outward(q, up, k).wait_recv()
                    if far < reach(q):
                        @pl.when(pos < length - 1 if up else pos > 0)
                        def _():
                            outward(q, up, k).start()
                    back(q, k, core).start()

            guarded(t - LAG * far, True, go)

        for far in range(reach(q), 0, -1):
            run(far, True)
            run(far, False)

    def sent(q, k):
        pos, length, _ = teeth[q]
        at, span, _ = spine[q]
        across(q, k).wait_send()
        back(q, k, core).wait_send()
        if length > 1:
            @pl.when(pos < root(q, k))
            def _():
                toward(q, True, k).wait_send()

            @pl.when(pos > root(q, k))
            def _():
                toward(q, False, k).wait_send()

            @pl.when((pos >= root(q, k)) & (pos < length - 1))
            def _():
                outward(q, True, k).wait_send()

            @pl.when((pos <= root(q, k)) & (pos > 0))
            def _():
                outward(q, False, k).wait_send()
        if span > 1:
            @pl.when((pos == root(q, k)) & (at < span - 1))
            def _():
                onward(q, True, k, own.at[q, k]).wait_send()

            @pl.when((pos == root(q, k)) & (at > 0))
            def _():
                onward(q, False, k, own.at[q, k]).wait_send()

    sign = jnp.where(lax.broadcasted_iota(jnp.int32, (1, depth), 1) < nwin, -1.0, 1.0)

    def settle(k):
        b, pair = k // per, k % per
        base = (b % 2) * (2 * nsrc * pitch)
        for q in range(2):
            back(q, k, 1 - core).wait_recv()
        for q in range(2):
            at = spot(q, k, 0)
            x = jnp.transpose(jnp.concatenate([gathered[at], gathered[at + 1]], axis=0)).astype(jnp.float32)
            s = 2 * pair + q
            src_t[pl.ds(base + s * pitch, FB)] = x
            src_t[pl.ds(base + (s + nsrc) * pitch, FB)] = pltpu.roll(x, nwin, axis=1) * sign
        for q in range(2):
            sent(q, k)

    def turn(k):
        b, lot = k // per, k % per
        base = (b % 3) * (nrow * pitch)
        count = nchan // per
        for u in range(count):
            c = lot * count + u
            x = jnp.transpose(spec[b, c]).astype(jnp.float32) * flags[pl.ds(c, 1)]
            chan_t[pl.ds(base + (c + HALO) * pitch, FB)] = x

        @pl.when(lot == 0)
        def _():
            column = pl.multiple_of(b * FB, FB)
            for h in range(2 * HALO):
                row = halo_valid[h // HALO][(8 - HALO + h) if h < HALO else (h - HALO)][None].astype(jnp.float32)
                row = jnp.concatenate([row, row], axis=1)
                x = jnp.transpose(halo[h, :, pl.ds(column, FB)]).astype(jnp.float32) * row
                c = h if h < HALO else nchan + h
                chan_t[pl.ds(base + c * pitch, FB)] = x

    def correlate(b, f):
        right = chan_t[pl.ds((b % 3) * (nrow * pitch) + f, nrow, stride=pitch)].astype(jnp.bfloat16)
        left = src_t[pl.ds((b % 2) * (2 * nsrc * pitch) + f, 2 * nsrc, stride=pitch)].astype(jnp.bfloat16)
        both = lax.dot_general(left, right, (((1,), (1,)), ((), ())), preferred_element_type=jnp.float32)
        cross_t[pl.ds((b % 2) * (FB * cpitch) + f * cpitch, 2 * nsrc), 0:nrow] = both

    ahead = (lax.broadcasted_iota(jnp.int32, (nchan, FB), 1)
             - lax.broadcasted_iota(jnp.int32, (nchan, FB), 0))
    band = ((ahead >= 0) & (ahead <= 2 * HALO)).astype(jnp.bfloat16)

    def smooth(b, s):
        base = (b % 2) * (FB * cpitch)
        re = cross_t[pl.ds(base + s, FB, stride=cpitch)]
        im = cross_t[pl.ds(base + s + nsrc, FB, stride=cpitch)]
        flat = jnp.concatenate([re, im], axis=0).astype(jnp.bfloat16)
        total = lax.dot_general(band, flat, (((1,), (1,)), ((), ())),
                                preferred_element_type=jnp.float32).astype(jnp.bfloat16)
        rows = pl.ds(pl.multiple_of(s * nchan, nchan), nchan)
        flat_ref[rows, pl.ds(pl.multiple_of(b * FB, FB), FB)] = total[:, 0:FB]
        flat_ref[rows, pl.ds(pl.multiple_of((nblk + b) * FB, FB), FB)] = total[:, FB:]

    load_first.wait()

    def prepare_first(k, carry):
        for q in range(2):
            prepare(first, 2 * k + q, q, k)
        return carry

    lax.fori_loop(0, per, prepare_first, 0, unroll=True)

    @pl.when(me == 0)
    def _():
        halo[0:HALO] = jnp.zeros((HALO,) + halo.shape[1:], halo.dtype)
        halo_valid[0] = jnp.zeros(halo_valid.shape[1:], halo_valid.dtype)

    @pl.when(me == size - 1)
    def _():
        halo[HALO:] = jnp.zeros((HALO,) + halo.shape[1:], halo.dtype)
        halo_valid[1] = jnp.zeros(halo_valid.shape[1:], halo_valid.dtype)

    def step(t, carry):
        @pl.when(t == LOADED)
        def _():
            for b in range(nblk):
                load(b).wait()

        @pl.when(t == LOADED + 1)
        def _():
            cross_t[...] = jnp.zeros(cross_t.shape, cross_t.dtype)
            pads = (nrow - nchan - 2 * HALO) * pitch
            for slot in range(3):
                chan_t[slot * nrow * pitch + (nrow * pitch - pads):(slot + 1) * nrow * pitch] = (
                    jnp.zeros((pads, depth), jnp.float32))

        @pl.when(t == turn_at)
        def _():
            @pl.when(me > 0)
            def _():
                for copy in edges(True):
                    copy.wait_recv()

            @pl.when(me < size - 1)
            def _():
                for copy in edges(False):
                    copy.wait_recv()

        for q in range(2):
            spread(q, t - summed[q])
            relay_on(q, t - rooted[q])
            guarded(t - summed[q], True, functools.partial(finish, q))
            guarded(t - rooted[q], True, functools.partial(reach_root, q))
            relay_in(q, t - ENTER)
            guarded(t - ENTER, True, functools.partial(enter, q))

        def prepare_later(k):
            for q in range(2):
                s = 2 * (k % per) + q
                prepare(spec.at[k // per], s, q, k)

        guarded(t, t >= per, prepare_later)
        guarded(t - turn_at, True, turn)
        guarded(t - settled, True, settle)

        at = t - settled - per

        @pl.when((at >= 0) & (at < n - per))
        def _():
            b, lot = at // per, at % per
            for u in range(FB // per):
                correlate(b, lot * (FB // per) + u)

        also = at - per

        @pl.when((also >= 0) & (also < n - 2 * per))
        def _():
            b, lot = also // per, also % per
            for u in range(2):
                smooth(b, lot * 2 + u)

        return carry

    lax.fori_loop(0, n + settled, step, 0)

    def rest(u, carry):
        for v in range(32):
            correlate(nblk - 1, u * 32 + v)
        return carry

    lax.fori_loop(0, FB // 32, rest, 0)
    for b in range(max(nblk - 2, 0), nblk):
        def last(s, carry):
            smooth(b, s)
            return carry

        lax.fori_loop(0, nsrc, last, 0, unroll=4)

    @pl.when(me < size - 1)
    def _():
        for copy in edges(True):
            copy.wait_send()

    @pl.when(me > 0)
    def _():
        for copy in edges(False):
            copy.wait_send()


def lag_kernel(scale, flat_ref, table_ref, out_ref):
    lags = jnp.dot(flat_ref[...], table_ref[...], preferred_element_type=jnp.float32)
    out_ref[...] = lags * scale


def local(size, spectra, valid, sources):
    nchan, _, nwin, nbins = spectra.shape
    nsrc = sources.shape[0]
    depth, nlags = 2 * nwin, 2 * nbins
    spec = spectra.reshape(nchan, depth, nbins)
    vmem = pl.BlockSpec(memory_space=pltpu.VMEM)

    chips = size // 2
    inner = 1
    while (2 * inner) ** 2 <= chips and chips % (2 * inner) == 0:
        inner *= 2
    outer = chips // inner
    nblk = nbins // FB
    n = nblk * nsrc // 2
    nrow = -(-(nchan + 2 * HALO) // 16) * 16
    pitch, cpitch = FB + 1, 2 * nsrc + 1
    chunks = lambda *lead: pltpu.VMEM(lead + (2, n, nwin, FB), jnp.bfloat16)
    flat = pl.pallas_call(
        functools.partial(cross_kernel, outer, inner, nrow),
        out_shape=jax.ShapeDtypeStruct((nsrc * nchan, nlags), jnp.bfloat16),
        in_specs=[pl.BlockSpec(memory_space=pltpu.SMEM), vmem, pl.BlockSpec(memory_space=pltpu.MemorySpace.HBM)],
        out_specs=vmem,
        scratch_shapes=[pltpu.VMEM((nchan, depth, FB), jnp.bfloat16),
                        pltpu.VMEM((nblk, nchan, depth, FB), jnp.bfloat16),
                        pltpu.VMEM((2 * HALO, depth, nbins), jnp.bfloat16),
                        pltpu.VMEM((2, 8, nwin), jnp.int32),
                        pltpu.VMEM((nchan, depth), jnp.float32),
                        pltpu.VMEM((nsrc, nwin, FB), jnp.bfloat16),
                        chunks(), chunks(), chunks(), chunks(2), chunks(2), chunks(2),
                        pltpu.VMEM((nblk * nsrc * 2, nwin, FB), jnp.bfloat16),
                        pltpu.VMEM((3 * nrow * pitch, depth), jnp.float32),
                        pltpu.VMEM((2 * 2 * nsrc * pitch, depth), jnp.float32),
                        pltpu.VMEM((2 * FB * cpitch, FB), jnp.float32),
                        pltpu.SemaphoreType.DMA((1 + nblk,)),
                        pltpu.SemaphoreType.DMA((KINDS, 2, n)), pltpu.SemaphoreType.DMA((KINDS, 2, n)),
                        pltpu.SemaphoreType.DMA((2, 2)), pltpu.SemaphoreType.DMA((2, 2))],
        compiler_params=pltpu.CompilerParams(
            collective_id=0, has_side_effects=True, vmem_limit_bytes=54 << 20),
        name="cross",
    )(sources, valid, spec)

    rows = nsrc * nchan // 4
    lags = pl.pallas_call(
        functools.partial(lag_kernel, 1.0 / (nwin * (2 * HALO + 1.0))),
        grid=(4,),
        out_shape=jax.ShapeDtypeStruct((nsrc * nchan, nlags), jnp.float32),
        in_specs=[pl.BlockSpec((rows, nlags), lambda at: (at, 0)),
                  pl.BlockSpec((nlags, nlags), lambda at: (0, 0))],
        out_specs=pl.BlockSpec((rows, nlags), lambda at: (at, 0)),
        compiler_params=pltpu.CompilerParams(vmem_limit_bytes=24 << 20),
        name="lags",
    )(flat, jnp.asarray(make_table(nbins, nlags)))
    return lags.reshape(nsrc, nchan, nlags)


def solution(mesh):
    in_specs = (P(("grp", "chan"), None, None, None), P(("grp", "chan"), None), P("grp"))
    out_specs = P("grp", "chan", None)
    return jax.shard_map(functools.partial(local, mesh.shape["chan"]), mesh=mesh,
                         in_specs=in_specs, out_specs=out_specs, check_vma=False)
```

```python
import functools

import jax
import jax.numpy as jnp
import numpy as np
from jax import lax
from jax.experimental import pallas as pl
from jax.experimental.pallas import tpu as pltpu
from jax.sharding import PartitionSpec as P

MESH = pl.DeviceIdType.MESH
HALO = 2
LAG = 3
ENTER = 2
SETTLE = 2
LOADED = 4
EARLY = 5
FB = 128
MANY = 2
IN_UP, IN_DOWN, ON_UP, ON_DOWN, OUT_UP, OUT_DOWN = range(6)


def make_table(nbins, nlags):
    freq = np.arange(nbins, dtype=np.int64)
    phase = (freq[:, None] * np.arange(nlags, dtype=np.int64)[None, :]) % nlags
    angle = 2.0 * np.pi * phase / nlags
    weight = np.where(freq == 0, 1.0, 2.0) / nlags
    table = np.concatenate([weight[:, None] * np.cos(angle), -weight[:, None] * np.sin(angle)])
    return table.astype(np.float32).astype(jnp.bfloat16)


def cross_kernel(outer, inner, nrow, src_ref, valid_ref, spec_ref, flat_ref,
                 first, spec, halo, halo_valid, flags, plane, give, own, part, inward, along, passed, gathered,
                 chan_t, src_t, cross_t, load_sem, pair_send, pair_recv, send_sem, recv_sem, edge_send, edge_recv):
    nblk, nchan, _, nwin, _ = spec.shape
    nsrc, depth = plane.shape[0], 2 * nwin
    n, _, many, _, _ = give.shape
    per = n // nblk
    size = outer * inner * 2
    me = lax.axis_index("chan")
    core, chip = me % 2, me // 2
    j, i = chip % inner, chip // inner
    line_j, line_i = (j, inner, 2), (i, outer, 2 * inner)
    teeth, spine = (line_j, line_i), (line_i, line_j)
    partner = me + 1 - 2 * core
    pitch, cpitch = FB + 1, 2 * nsrc + 1

    def root(q, odd):
        length = teeth[q][1]
        return 0 if length == 1 else (length - 1) // 2 + odd

    reach = [max(root(q, 1), teeth[q][1] - 1 - root(q, 0)) for q in range(2)]
    rooted = [ENTER + LAG * reach[q] for q in range(2)]
    summed = [rooted[q] + LAG * (spine[q][1] - 1) for q in range(2)]
    spread_at = max(summed[q] + LAG * reach[q] for q in range(2))
    settled = spread_at + SETTLE
    turn_at = settled - per
    at_root = [[teeth[q][0] == root(q, odd) for odd in range(2)] for q in range(2)]

    def load(b):
        return pltpu.make_async_copy(spec_ref.at[:, :, :, pl.ds(b * FB, FB)], spec.at[b], load_sem.at[1 + b])

    load_first = pltpu.make_async_copy(spec_ref.at[:, :, :, pl.ds(0, FB)], first, load_sem.at[0])
    load_first.start()
    for b in range(nblk):
        load(b).start()

    barrier = pltpu.get_barrier_semaphore()

    def greet(there):
        pl.semaphore_signal(barrier, inc=1, device_id={"chan": there}, device_id_type=MESH)

    greet(partner)
    count = jnp.int32(1)
    for pos, length, stride in (line_j, line_i, (me, size, 1)):
        @pl.when(pos > 0)
        def _():
            greet(me - stride)

        @pl.when(pos < length - 1)
        def _():
            greet(me + stride)

        count = count + (pos > 0).astype(jnp.int32) + (pos < length - 1).astype(jnp.int32)

    raw = valid_ref[...].astype(jnp.float32)
    flags[...] = jnp.concatenate([raw, raw], axis=1)
    by_window = jnp.transpose(flags[...])[0:nwin].astype(jnp.bfloat16)
    place = lax.broadcasted_iota(jnp.int32, (nchan, FB), 0)
    for s in range(nsrc):
        hot = (place == src_ref[s] - me * nchan).astype(jnp.bfloat16)
        plane[s] = jnp.dot(by_window, hot, preferred_element_type=jnp.float32).astype(jnp.bfloat16)

    pl.semaphore_wait(barrier, count)

    def edge_flags(up):
        side, eight = (0, nchan - 8) if up else (1, 0)
        return pltpu.make_async_remote_copy(
            src_ref=valid_ref.at[pl.ds(eight, 8)], dst_ref=halo_valid.at[side],
            send_sem=edge_send.at[side, nblk], recv_sem=edge_recv.at[side, nblk],
            device_id={"chan": me + 1 if up else me - 1}, device_id_type=MESH)

    def edge(up, b):
        side, rows = (0, nchan - HALO) if up else (1, 0)
        return pltpu.make_async_remote_copy(
            src_ref=spec_ref.at[pl.ds(rows, HALO), :, :, pl.ds(b * FB, FB)], dst_ref=halo.at[side, b],
            send_sem=edge_send.at[side, b], recv_sem=edge_recv.at[side, b],
            device_id={"chan": me + 1 if up else me - 1}, device_id_type=MESH)

    def to_neighbours(act, blocks=()):
        @pl.when(me < size - 1)
        def _():
            for copy in [edge(True, b) for b in blocks] or [edge_flags(True)]:
                act(copy)

        @pl.when(me > 0)
        def _():
            for copy in [edge(False, b) for b in blocks] or [edge_flags(False)]:
                act(copy)

    def from_neighbours(blocks=()):
        @pl.when(me > 0)
        def _():
            for copy in [edge(True, b) for b in blocks] or [edge_flags(True)]:
                copy.wait_recv()

        @pl.when(me < size - 1)
        def _():
            for copy in [edge(False, b) for b in blocks] or [edge_flags(False)]:
                copy.wait_recv()

    to_neighbours(lambda copy: copy.start())

    def across(k):
        return pltpu.make_async_remote_copy(
            src_ref=give.at[k], dst_ref=part.at[k], send_sem=pair_send.at[0], recv_sem=pair_recv.at[0, k],
            device_id={"chan": partner}, device_id_type=MESH)

    def back(k, half):
        return pltpu.make_async_remote_copy(
            src_ref=gathered.at[k, half], dst_ref=gathered.at[k, half], send_sem=pair_send.at[1],
            recv_sem=pair_recv.at[1, k], device_id={"chan": partner}, device_id_type=MESH)

    def remote(src, dst, kind, q, odd, k, there):
        return pltpu.make_async_remote_copy(
            src_ref=src, dst_ref=dst, send_sem=send_sem.at[kind, q, odd], recv_sem=recv_sem.at[kind, q, k],
            device_id={"chan": there}, device_id_type=MESH)

    def toward(q, up, odd, k):
        there = me + teeth[q][2] if up else me - teeth[q][2]
        return remote(own.at[k, q], inward.at[0 if up else 1, k, q], IN_UP if up else IN_DOWN, q, odd, k, there)

    def onward(q, up, odd, k, src):
        there = me + spine[q][2] if up else me - spine[q][2]
        return remote(src, along.at[0 if up else 1, k, q], ON_UP if up else ON_DOWN, q, odd, k, there)

    def outward(q, up, odd, k):
        there = me + teeth[q][2] if up else me - teeth[q][2]
        block = gathered.at[k, core, q]
        return remote(block, block, OUT_UP if up else OUT_DOWN, q, odd, k, there)

    def prepare(block, k):
        for q in range(2):
            for m in range(many):
                s = ((k % per) * 2 + q) * many + m
                held = jnp.clip(src_ref[s] - me * nchan, 0, nchan - 1)
                mask = plane[s]
                give[k, q, m] = block[held, 1 - core] * mask
                own[k, q, m] = block[held, core] * mask
        across(k).start()

    def guarded(k, also, run):
        @pl.when((k >= 0) & (k < n) & also)
        def _():
            run()

    def enter(k, odd):
        across(k).wait_recv()
        own[k] = own[k] + part[k]
        for q in range(2):
            pos, length, _ = teeth[q]
            if root(q, odd) > 0:
                @pl.when(pos == 0)
                def _():
                    toward(q, True, odd, k).start()

            if root(q, odd) < length - 1:
                @pl.when(pos == length - 1)
                def _():
                    toward(q, False, odd, k).start()

    def relay_in(q, t, p):
        pos, length, _ = teeth[q]
        for up in (True, False):
            for here in range(1, length - 1):
                steps = here if up else length - 1 - here
                odd = (p - LAG * steps) % 2
                k = t - LAG * steps
                if (here < root(q, odd)) if up else (here > root(q, odd)):
                    def run():
                        toward(q, up, odd, k).wait_recv()
                        own[k, q] = own[k, q] + inward[0 if up else 1, k, q]
                        toward(q, up, odd, k).start()

                    guarded(k, pos == here, run)

    def reach_root(q, k, odd):
        length = teeth[q][1]
        at, span, _ = spine[q]
        ways = []
        if root(q, odd) > 0:
            ways.append(0)
        if root(q, odd) < length - 1:
            ways.append(1)
        for way in ways:
            toward(q, way == 0, odd, k).wait_recv()
        if ways:
            total = own[k, q]
            for way in ways:
                total = total + inward[way, k, q]
            own[k, q] = total
        if span > 1:
            @pl.when(at == 0)
            def _():
                onward(q, True, odd, k, own.at[k, q]).start()

            @pl.when(at == span - 1)
            def _():
                onward(q, False, odd, k, own.at[k, q]).start()

    def relay_on(q, t, p):
        at, span, _ = spine[q]
        for up in (True, False):
            for here in range(1, span - 1):
                steps = here if up else span - 1 - here
                odd = (p - LAG * steps) % 2
                k = t - LAG * steps

                def run():
                    way = 0 if up else 1
                    onward(q, up, odd, k, own.at[k, q]).wait_recv()
                    passed[way, k, q] = own[k, q] + along[way, k, q]
                    onward(q, up, odd, k, passed.at[way, k, q]).start()

                guarded(k, at_root[q][odd] & (at == here), run)

    def finish(q, k, odd):
        pos, length, _ = teeth[q]
        at, span, _ = spine[q]
        if span == 1:
            gathered[k, core, q] = own[k, q]
        else:
            @pl.when(at == 0)
            def _():
                onward(q, False, odd, k, own.at[k, q]).wait_recv()
                gathered[k, core, q] = own[k, q] + along[1, k, q]

            @pl.when(at == span - 1)
            def _():
                onward(q, True, odd, k, own.at[k, q]).wait_recv()
                gathered[k, core, q] = own[k, q] + along[0, k, q]

            if span > 2:
                @pl.when((at > 0) & (at < span - 1))
                def _():
                    gathered[k, core, q] = own[k, q] + along[0, k, q] + along[1, k, q]
        if root(q, odd) < length - 1:
            outward(q, True, odd, k).start()
        if root(q, odd) > 0:
            outward(q, False, odd, k).start()

    def spread(q, t, p):
        pos, length, _ = teeth[q]
        for far in range(reach[q], 0, -1):
            odd = (p - LAG * far) % 2
            k = t - LAG * far
            for up in (True, False):
                here = root(q, odd) + far if up else root(q, odd) - far
                if 0 <= here < length:
                    def run():
                        outward(q, up, odd, k).wait_recv()
                        if (here < length - 1) if up else (here > 0):
                            outward(q, up, odd, k).start()

                    guarded(k, pos == here, run)

    def all_sent():
        def drain(block, sem):
            pltpu.make_async_remote_copy(
                src_ref=block, dst_ref=block, send_sem=sem, recv_sem=pair_recv.at[0, 0],
                device_id={"chan": partner}, device_id_type=MESH).wait_send()

        drain(give, pair_send.at[0])
        drain(give, pair_send.at[1])
        for q in range(2):
            pos, length, _ = teeth[q]
            at, span, _ = spine[q]
            for odd in range(2):
                r = root(q, odd)
                for kind, when in ((IN_UP, pos < r), (IN_DOWN, pos > r),
                                   (ON_UP, (pos == r) & (at < span - 1)), (ON_DOWN, (pos == r) & (at > 0)),
                                   (OUT_UP, (pos >= r) & (pos < length - 1)), (OUT_DOWN, (pos <= r) & (pos > 0))):
                    @pl.when(when)
                    def _():
                        drain(own.at[pl.ds(0, n // 2), q], send_sem.at[kind, q, odd])

    sign = jnp.where(lax.broadcasted_iota(jnp.int32, (1, depth), 1) < nwin, -1.0, 1.0)

    def settle(k):
        base = ((k // per) % 2) * (2 * nsrc * pitch)
        back(k, 1 - core).wait_recv()
        for q in range(2):
            for m in range(many):
                both = jnp.concatenate([gathered[k, 0, q, m], gathered[k, 1, q, m]], axis=0)
                x = jnp.transpose(both).astype(jnp.float32)
                s = ((k % per) * 2 + q) * many + m
                src_t[pl.ds(base + s * pitch, FB)] = x
                src_t[pl.ds(base + (s + nsrc) * pitch, FB)] = pltpu.roll(x, nwin, axis=1) * sign

    def turn(k):
        b, lot = k // per, k % per
        base = (b % 3) * (nrow * pitch)
        count = nchan // per
        for u in range(count):
            c = lot * count + u
            x = jnp.transpose(spec[b, c].reshape(depth, FB)).astype(jnp.float32) * flags[pl.ds(c, 1)]
            chan_t[pl.ds(base + (c + HALO) * pitch, FB)] = x

    def turn_edges(b):
        from_neighbours([b])
        base = (b % 3) * (nrow * pitch)
        for h in range(2 * HALO):
            side, c = h // HALO, h % HALO
            row = halo_valid[side][(8 - HALO + c) if side == 0 else c][None].astype(jnp.float32)
            row = jnp.concatenate([row, row], axis=1)
            x = jnp.transpose(halo[side, b, c].reshape(depth, FB)).astype(jnp.float32) * row
            chan_t[pl.ds(base + (c + side * (HALO + nchan)) * pitch, FB)] = x

    def correlate(b, f):
        right = chan_t[pl.ds((b % 3) * (nrow * pitch) + f, nrow, stride=pitch)].astype(jnp.bfloat16)
        left = src_t[pl.ds((b % 2) * (2 * nsrc * pitch) + f, 2 * nsrc, stride=pitch)].astype(jnp.bfloat16)
        both = lax.dot_general(left, right, (((1,), (1,)), ((), ())), preferred_element_type=jnp.float32)
        cross_t[pl.ds((b % 2) * (FB * cpitch) + f * cpitch, 2 * nsrc), 0:nrow] = both

    ahead = (lax.broadcasted_iota(jnp.int32, (nchan, FB), 1)
             - lax.broadcasted_iota(jnp.int32, (nchan, FB), 0))
    band = ((ahead >= 0) & (ahead <= 2 * HALO)).astype(jnp.bfloat16)

    def smooth(b, s):
        base = (b % 2) * (FB * cpitch)
        re = cross_t[pl.ds(base + s, FB, stride=cpitch)]
        im = cross_t[pl.ds(base + s + nsrc, FB, stride=cpitch)]
        flat = jnp.concatenate([re, im], axis=0).astype(jnp.bfloat16)
        total = lax.dot_general(band, flat, (((1,), (1,)), ((), ())),
                                preferred_element_type=jnp.float32).astype(jnp.bfloat16)
        rows = pl.ds(pl.multiple_of(s * nchan, nchan), nchan)
        flat_ref[rows, pl.ds(pl.multiple_of(b * FB, FB), FB)] = total[:, 0:FB]
        flat_ref[rows, pl.ds(pl.multiple_of((nblk + b) * FB, FB), FB)] = total[:, FB:]

    load_first.wait()

    def prepare_first(k, carry):
        prepare(first, k)
        return carry

    lax.fori_loop(0, per, prepare_first, 0, unroll=True)

    @pl.when(me == 0)
    def _():
        halo[0] = jnp.zeros(halo.shape[1:], halo.dtype)
        halo_valid[0] = jnp.zeros(halo_valid.shape[1:], halo_valid.dtype)

    @pl.when(me == size - 1)
    def _():
        halo[1] = jnp.zeros(halo.shape[1:], halo.dtype)
        halo_valid[1] = jnp.zeros(halo_valid.shape[1:], halo_valid.dtype)

    def clear():
        def some(f, carry):
            cross_t[pl.ds(pl.multiple_of(f * 8 * cpitch, 8), 8 * cpitch)] = jnp.zeros((8 * cpitch, FB), jnp.float32)
            return carry

        lax.fori_loop(0, 2 * FB // 8, some, 0)
        for slot in range(3):
            for c in range(nchan + 2 * HALO, nrow):
                chan_t[pl.ds((slot * nrow + c) * pitch, pitch)] = jnp.zeros((pitch, depth), jnp.float32)

    def step(t, p):
        @pl.when(t == LOADED)
        def _():
            for b in range(nblk):
                load(b).wait()

        @pl.when(t == LOADED + 1)
        def _():
            clear()
            from_neighbours()

        for b in range(nblk):
            @pl.when(t == settled + per * (b + 1) - EARLY)
            def _():
                to_neighbours(lambda copy: copy.start(), [b])

        guarded(t - ENTER, True, functools.partial(enter, t - ENTER, (p - ENTER) % 2))
        for q in range(2):
            relay_in(q, t - ENTER, (p - ENTER) % 2)
        for q in range(2):
            odd = (p - rooted[q]) % 2
            guarded(t - rooted[q], at_root[q][odd], functools.partial(reach_root, q, t - rooted[q], odd))
        for q in range(2):
            relay_on(q, t - rooted[q], (p - rooted[q]) % 2)
        for q in range(2):
            odd = (p - summed[q]) % 2
            guarded(t - summed[q], at_root[q][odd], functools.partial(finish, q, t - summed[q], odd))
        for q in range(2):
            spread(q, t - summed[q], (p - summed[q]) % 2)
        guarded(t - spread_at, True, lambda: back(t - spread_at, core).start())
        guarded(t, t >= per, lambda: prepare(spec.at[t // per], t))
        guarded(t - turn_at, True, functools.partial(turn, t - turn_at))
        guarded(t - settled, True, functools.partial(settle, t - settled))

        for b in range(nblk):
            @pl.when(t == settled + per * (b + 1) - 1)
            def _():
                turn_edges(b)

        at = t - settled - per

        @pl.when((at >= 0) & (at < n - per))
        def _():
            b, lot = at // per, at % per
            for u in range(FB // per):
                correlate(b, lot * (FB // per) + u)

        also = at - per

        @pl.when((also >= 0) & (also < n - 2 * per))
        def _():
            b, lot = also // per, also % per
            for u in range(nsrc // per):
                smooth(b, lot * (nsrc // per) + u)

    def steps(tt, carry):
        for p in range(2):
            step(2 * tt + p, p)
        return carry

    lax.fori_loop(0, (n + settled + 1) // 2, steps, 0)

    def rest(u, carry):
        for v in range(32):
            correlate(nblk - 1, u * 32 + v)
        return carry

    lax.fori_loop(0, FB // 32, rest, 0)
    for b in range(max(nblk - 2, 0), nblk):
        def last(s, carry):
            smooth(b, s)
            return carry

        lax.fori_loop(0, nsrc, last, 0, unroll=4)
    all_sent()
    to_neighbours(lambda copy: copy.wait_send())
    to_neighbours(lambda copy: copy.wait_send(), range(nblk))


def lag_kernel(scale, flat_ref, table_ref, out_ref):
    lags = jnp.dot(flat_ref[...], table_ref[...], preferred_element_type=jnp.float32)
    out_ref[...] = lags * scale


def local(size, spectra, valid, sources):
    nchan, _, nwin, nbins = spectra.shape
    nsrc = sources.shape[0]
    depth, nlags = 2 * nwin, 2 * nbins
    vmem = pl.BlockSpec(memory_space=pltpu.VMEM)

    chips = size // 2
    inner = 1
    while (2 * inner) ** 2 <= chips and chips % (2 * inner) == 0:
        inner *= 2
    outer = chips // inner
    nblk = nbins // FB
    many = MANY
    n = nblk * nsrc // (2 * many)
    nrow = -(-(nchan + 2 * HALO) // 16) * 16
    pitch, cpitch = FB + 1, 2 * nsrc + 1
    chunks = lambda *lead: pltpu.VMEM(lead + (n, 2, many, nwin, FB), jnp.bfloat16)
    flat = pl.pallas_call(
        functools.partial(cross_kernel, outer, inner, nrow),
        out_shape=jax.ShapeDtypeStruct((nsrc * nchan, nlags), jnp.bfloat16),
        in_specs=[pl.BlockSpec(memory_space=pltpu.SMEM), vmem, pl.BlockSpec(memory_space=pltpu.MemorySpace.HBM)],
        out_specs=vmem,
        scratch_shapes=[pltpu.VMEM((nchan, 2, nwin, FB), jnp.bfloat16),
                        pltpu.VMEM((nblk, nchan, 2, nwin, FB), jnp.bfloat16),
                        pltpu.VMEM((2, nblk, HALO, 2, nwin, FB), jnp.bfloat16),
                        pltpu.VMEM((2, 8, nwin), jnp.int32),
                        pltpu.VMEM((nchan, depth), jnp.float32),
                        pltpu.VMEM((nsrc, nwin, FB), jnp.bfloat16),
                        chunks(), chunks(), chunks(), chunks(2), chunks(2), chunks(2),
                        pltpu.VMEM((n, 2, 2, many, nwin, FB), jnp.bfloat16),
                        pltpu.VMEM((3 * nrow * pitch, depth), jnp.float32),
                        pltpu.VMEM((2 * 2 * nsrc * pitch, depth), jnp.float32),
                        pltpu.VMEM((2 * FB * cpitch, FB), jnp.float32),
                        pltpu.SemaphoreType.DMA((1 + nblk,)),
                        pltpu.SemaphoreType.DMA((2,)), pltpu.SemaphoreType.DMA((2, n)),
                        pltpu.SemaphoreType.DMA((6, 2, 2)), pltpu.SemaphoreType.DMA((6, 2, n)),
                        pltpu.SemaphoreType.DMA((2, nblk + 1)), pltpu.SemaphoreType.DMA((2, nblk + 1))],
        compiler_params=pltpu.CompilerParams(
            collective_id=0, has_side_effects=True, vmem_limit_bytes=54 << 20),
        name="cross",
    )(sources, valid, spectra)

    rows = nsrc * nchan // 4
    lags = pl.pallas_call(
        functools.partial(lag_kernel, 1.0 / (nwin * (2 * HALO + 1.0))),
        grid=(4,),
        out_shape=jax.ShapeDtypeStruct((nsrc * nchan, nlags), jnp.float32),
        in_specs=[pl.BlockSpec((rows, nlags), lambda at: (at, 0)),
                  pl.BlockSpec((nlags, nlags), lambda at: (0, 0))],
        out_specs=pl.BlockSpec((rows, nlags), lambda at: (at, 0)),
        compiler_params=pltpu.CompilerParams(vmem_limit_bytes=24 << 20),
        name="lags",
    )(flat, jnp.asarray(make_table(nbins, nlags)))
    return lags.reshape(nsrc, nchan, nlags)


def solution(mesh):
    in_specs = (P(("grp", "chan"), None, None, None), P(("grp", "chan"), None), P("grp"))
    out_specs = P("grp", "chan", None)
    return jax.shard_map(functools.partial(local, mesh.shape["chan"]), mesh=mesh,
                         in_specs=in_specs, out_specs=out_specs, check_vma=False)
```

```python
import functools

import jax
import jax.numpy as jnp
import numpy as np
from jax import lax
from jax.experimental import pallas as pl
from jax.experimental.pallas import tpu as pltpu
from jax.sharding import PartitionSpec as P

MESH = pl.DeviceIdType.MESH
HALO = 2
LAG = 3
AHEAD = 2
SETTLE = 2
EARLY = 5
FB = 128
MANY = 2
IN_UP, IN_DOWN, ON_UP, ON_DOWN, OUT_UP, OUT_DOWN = range(6)


def make_table(nbins, nlags):
    freq = np.arange(nbins, dtype=np.int64)
    phase = (freq[:, None] * np.arange(nlags, dtype=np.int64)[None, :]) % nlags
    angle = 2.0 * np.pi * phase / nlags
    weight = np.where(freq == 0, 1.0, 2.0) / nlags
    table = np.concatenate([weight[:, None] * np.cos(angle), -weight[:, None] * np.sin(angle)])
    order = np.concatenate([blk * FB + half * nbins + np.arange(odd, FB, 2)
                            for odd in range(2) for blk in range(nbins // FB) for half in range(2)])
    return table[order, :nlags // 2].astype(np.float32).astype(jnp.bfloat16)


def cross_kernel(outer, inner, nrow, src_ref, valid_ref, spec_ref, flat_ref,
                 first, spec, halo, halo_valid, flags, plane, give, own, part, inward, along, passed, gathered,
                 chan_t, src_t, cross_t, load_sem, pair_send, pair_recv, send_sem, recv_sem, edge_send, edge_recv):
    nblk, nchan, _, nwin, _ = spec.shape
    nsrc, depth = plane.shape[0], 2 * nwin
    n, _, many, _, _ = give.shape
    per = n // nblk
    size = outer * inner * 2
    me = lax.axis_index("chan")
    core, chip = me % 2, me // 2
    j, i = chip % inner, chip // inner
    line_j, line_i = (j, inner, 2), (i, outer, 2 * inner)
    teeth, spine = (line_j, line_i), (line_i, line_j)
    partner = me + 1 - 2 * core
    pitch, cpitch = FB + 1, 2 * nsrc + 1

    def root(q, odd):
        length = teeth[q][1]
        return 0 if length == 1 else (length - 1) // 2 + odd

    reach = [max(root(q, 1), teeth[q][1] - 1 - root(q, 0)) for q in range(2)]
    rooted = [LAG * reach[q] for q in range(2)]
    summed = [rooted[q] + LAG * (spine[q][1] - 1) for q in range(2)]
    spread_at = max(summed[q] + LAG * reach[q] for q in range(2))
    settled = spread_at + SETTLE
    loaded = max(per - AHEAD, 0)
    turn_at = min(loaded + 1, settled)
    at_root = [[teeth[q][0] == root(q, odd) for odd in range(2)] for q in range(2)]

    def load(b):
        return pltpu.make_async_copy(spec_ref.at[:, :, :, pl.ds(b * FB, FB)], spec.at[b], load_sem.at[1 + b])

    load_first = pltpu.make_async_copy(spec_ref.at[:, :, :, pl.ds(0, FB)], first, load_sem.at[0])
    load_first.start()
    for b in range(nblk):
        load(b).start()

    barrier = pltpu.get_barrier_semaphore()

    def greet(there):
        pl.semaphore_signal(barrier, inc=1, device_id={"chan": there}, device_id_type=MESH)

    greet(partner)
    count = jnp.int32(1)
    for pos, length, stride in (line_j, line_i, (me, size, 1)):
        @pl.when(pos > 0)
        def _():
            greet(me - stride)

        @pl.when(pos < length - 1)
        def _():
            greet(me + stride)

        count = count + (pos > 0).astype(jnp.int32) + (pos < length - 1).astype(jnp.int32)

    raw = valid_ref[...].astype(jnp.float32)
    flags[...] = jnp.concatenate([raw, raw], axis=1)
    by_window = jnp.transpose(flags[...])[0:nwin].astype(jnp.bfloat16)
    place = lax.broadcasted_iota(jnp.int32, (nchan, FB), 0)
    for s in range(nsrc):
        hot = (place == src_ref[s] - me * nchan).astype(jnp.bfloat16)
        plane[s] = jnp.dot(by_window, hot, preferred_element_type=jnp.float32).astype(jnp.bfloat16)

    pl.semaphore_wait(barrier, count)

    def edge_flags(up):
        side, eight = (0, nchan - 8) if up else (1, 0)
        return pltpu.make_async_remote_copy(
            src_ref=valid_ref.at[pl.ds(eight, 8)], dst_ref=halo_valid.at[side],
            send_sem=edge_send.at[side, nblk], recv_sem=edge_recv.at[side, nblk],
            device_id={"chan": me + 1 if up else me - 1}, device_id_type=MESH)

    def edge(up, b):
        side, rows = (0, nchan - HALO) if up else (1, 0)
        return pltpu.make_async_remote_copy(
            src_ref=spec_ref.at[pl.ds(rows, HALO), :, :, pl.ds(b * FB, FB)], dst_ref=halo.at[side, b],
            send_sem=edge_send.at[side, b], recv_sem=edge_recv.at[side, b],
            device_id={"chan": me + 1 if up else me - 1}, device_id_type=MESH)

    def to_neighbours(act, blocks=()):
        @pl.when(me < size - 1)
        def _():
            for copy in [edge(True, b) for b in blocks] or [edge_flags(True)]:
                act(copy)

        @pl.when(me > 0)
        def _():
            for copy in [edge(False, b) for b in blocks] or [edge_flags(False)]:
                act(copy)

    def from_neighbours(blocks=()):
        @pl.when(me > 0)
        def _():
            for copy in [edge(True, b) for b in blocks] or [edge_flags(True)]:
                copy.wait_recv()

        @pl.when(me < size - 1)
        def _():
            for copy in [edge(False, b) for b in blocks] or [edge_flags(False)]:
                copy.wait_recv()

    to_neighbours(lambda copy: copy.start())

    def across(k):
        return pltpu.make_async_remote_copy(
            src_ref=give.at[k], dst_ref=part.at[k], send_sem=pair_send.at[0], recv_sem=pair_recv.at[0, k],
            device_id={"chan": partner}, device_id_type=MESH)

    def back(k, half):
        return pltpu.make_async_remote_copy(
            src_ref=gathered.at[k, half], dst_ref=gathered.at[k, half], send_sem=pair_send.at[1],
            recv_sem=pair_recv.at[1, k], device_id={"chan": partner}, device_id_type=MESH)

    def remote(src, dst, kind, q, odd, k, there):
        return pltpu.make_async_remote_copy(
            src_ref=src, dst_ref=dst, send_sem=send_sem.at[kind, q, odd], recv_sem=recv_sem.at[kind, q, k],
            device_id={"chan": there}, device_id_type=MESH)

    def toward(q, up, odd, k):
        there = me + teeth[q][2] if up else me - teeth[q][2]
        return remote(own.at[k, q], inward.at[0 if up else 1, k, q], IN_UP if up else IN_DOWN, q, odd, k, there)

    def onward(q, up, odd, k, src):
        there = me + spine[q][2] if up else me - spine[q][2]
        return remote(src, along.at[0 if up else 1, k, q], ON_UP if up else ON_DOWN, q, odd, k, there)

    def outward(q, up, odd, k):
        there = me + teeth[q][2] if up else me - teeth[q][2]
        block = gathered.at[k, core, q]
        return remote(block, block, OUT_UP if up else OUT_DOWN, q, odd, k, there)

    def prepare(block, k):
        for q in range(2):
            for m in range(many):
                s = ((k % per) * 2 + q) * many + m
                held = jnp.clip(src_ref[s] - me * nchan, 0, nchan - 1)
                mask = plane[s]
                give[k, q, m] = block[held, 1 - core] * mask
                own[k, q, m] = block[held, core] * mask
        across(k).start()

    def guarded(k, also, run):
        @pl.when((k >= 0) & (k < n) & also)
        def _():
            run()

    def enter(k, odd):
        across(k).wait_recv()
        own[k] = own[k] + part[k]
        for q in range(2):
            pos, length, _ = teeth[q]
            if root(q, odd) > 0:
                @pl.when(pos == 0)
                def _():
                    toward(q, True, odd, k).start()

            if root(q, odd) < length - 1:
                @pl.when(pos == length - 1)
                def _():
                    toward(q, False, odd, k).start()

    def relay_in(q, t, p):
        pos, length, _ = teeth[q]
        for up in (True, False):
            for here in range(1, length - 1):
                steps = here if up else length - 1 - here
                odd = (p - LAG * steps) % 2
                k = t - LAG * steps
                if (here < root(q, odd)) if up else (here > root(q, odd)):
                    def run():
                        toward(q, up, odd, k).wait_recv()
                        own[k, q] = own[k, q] + inward[0 if up else 1, k, q]
                        toward(q, up, odd, k).start()

                    guarded(k, pos == here, run)

    def reach_root(q, k, odd):
        length = teeth[q][1]
        at, span, _ = spine[q]
        ways = []
        if root(q, odd) > 0:
            ways.append(0)
        if root(q, odd) < length - 1:
            ways.append(1)
        for way in ways:
            toward(q, way == 0, odd, k).wait_recv()
        if ways:
            total = own[k, q]
            for way in ways:
                total = total + inward[way, k, q]
            own[k, q] = total
        if span > 1:
            @pl.when(at == 0)
            def _():
                onward(q, True, odd, k, own.at[k, q]).start()

            @pl.when(at == span - 1)
            def _():
                onward(q, False, odd, k, own.at[k, q]).start()

    def relay_on(q, t, p):
        at, span, _ = spine[q]
        for up in (True, False):
            for here in range(1, span - 1):
                steps = here if up else span - 1 - here
                odd = (p - LAG * steps) % 2
                k = t - LAG * steps

                def run():
                    way = 0 if up else 1
                    onward(q, up, odd, k, own.at[k, q]).wait_recv()
                    passed[way, k, q] = own[k, q] + along[way, k, q]
                    onward(q, up, odd, k, passed.at[way, k, q]).start()

                guarded(k, at_root[q][odd] & (at == here), run)

    def finish(q, k, odd):
        pos, length, _ = teeth[q]
        at, span, _ = spine[q]
        if span == 1:
            gathered[k, core, q] = own[k, q]
        else:
            @pl.when(at == 0)
            def _():
                onward(q, False, odd, k, own.at[k, q]).wait_recv()
                gathered[k, core, q] = own[k, q] + along[1, k, q]

            @pl.when(at == span - 1)
            def _():
                onward(q, True, odd, k, own.at[k, q]).wait_recv()
                gathered[k, core, q] = own[k, q] + along[0, k, q]

            if span > 2:
                @pl.when((at > 0) & (at < span - 1))
                def _():
                    gathered[k, core, q] = own[k, q] + along[0, k, q] + along[1, k, q]
        if root(q, odd) < length - 1:
            outward(q, True, odd, k).start()
        if root(q, odd) > 0:
            outward(q, False, odd, k).start()

    def spread(q, t, p):
        pos, length, _ = teeth[q]
        for far in range(reach[q], 0, -1):
            odd = (p - LAG * far) % 2
            k = t - LAG * far
            for up in (True, False):
                here = root(q, odd) + far if up else root(q, odd) - far
                if 0 <= here < length:
                    def run():
                        outward(q, up, odd, k).wait_recv()
                        if (here < length - 1) if up else (here > 0):
                            outward(q, up, odd, k).start()

                    guarded(k, pos == here, run)

    def all_sent():
        def drain(block, sem):
            pltpu.make_async_remote_copy(
                src_ref=block, dst_ref=block, send_sem=sem, recv_sem=pair_recv.at[0, 0],
                device_id={"chan": partner}, device_id_type=MESH).wait_send()

        drain(give, pair_send.at[0])
        drain(give, pair_send.at[1])
        for q in range(2):
            pos, length, _ = teeth[q]
            at, span, _ = spine[q]
            for odd in range(2):
                r = root(q, odd)
                for kind, when in ((IN_UP, pos < r), (IN_DOWN, pos > r),
                                   (ON_UP, (pos == r) & (at < span - 1)), (ON_DOWN, (pos == r) & (at > 0)),
                                   (OUT_UP, (pos >= r) & (pos < length - 1)), (OUT_DOWN, (pos <= r) & (pos > 0))):
                    @pl.when(when)
                    def _():
                        drain(own.at[pl.ds(0, n // 2), q], send_sem.at[kind, q, odd])

    sign = jnp.where(lax.broadcasted_iota(jnp.int32, (1, depth), 1) < nwin, -1.0, 1.0)

    def settle(k):
        base = ((k // per) % 2) * (2 * nsrc * pitch)
        for q in range(2):
            for m in range(many):
                both = jnp.concatenate([gathered[k, 0, q, m], gathered[k, 1, q, m]], axis=0)
                x = jnp.transpose(both).astype(jnp.float32)
                s = ((k % per) * 2 + q) * many + m
                src_t[pl.ds(base + s * pitch, FB)] = x
                src_t[pl.ds(base + (s + nsrc) * pitch, FB)] = pltpu.roll(x, nwin, axis=1) * sign

    def turn(k):
        b, lot = k // per, k % per
        base = b * (nrow * pitch)
        count = nchan // per
        for u in range(count):
            c = lot * count + u
            x = jnp.transpose(spec[b, c].reshape(depth, FB)).astype(jnp.float32) * flags[pl.ds(c, 1)]
            chan_t[pl.ds(base + (c + HALO) * pitch, FB)] = x

    def turn_edges(b):
        from_neighbours([b])
        base = b * (nrow * pitch)
        for h in range(2 * HALO):
            side, c = h // HALO, h % HALO
            row = halo_valid[side][(8 - HALO + c) if side == 0 else c][None].astype(jnp.float32)
            row = jnp.concatenate([row, row], axis=1)
            x = jnp.transpose(halo[side, b, c].reshape(depth, FB)).astype(jnp.float32) * row
            chan_t[pl.ds(base + (c + side * (HALO + nchan)) * pitch, FB)] = x

    def correlate(b, f):
        right = chan_t[pl.ds(b * (nrow * pitch) + f, nrow, stride=pitch)].astype(jnp.bfloat16)
        left = src_t[pl.ds((b % 2) * (2 * nsrc * pitch) + f, 2 * nsrc, stride=pitch)].astype(jnp.bfloat16)
        both = lax.dot_general(left, right, (((1,), (1,)), ((), ())), preferred_element_type=jnp.float32)
        cross_t[pl.ds((b % 2) * (FB * cpitch) + f * cpitch, 2 * nsrc), 0:nrow] = both

    ahead = (lax.broadcasted_iota(jnp.int32, (nchan, FB), 1)
             - lax.broadcasted_iota(jnp.int32, (nchan, FB), 0))
    band = ((ahead >= 0) & (ahead <= 2 * HALO)).astype(jnp.bfloat16)

    def smooth(b, s):
        base = (b % 2) * (FB * cpitch)
        parts = [cross_t[pl.ds(base + odd * cpitch + s + half * nsrc, FB // 2, stride=2 * cpitch)]
                 for odd in range(2) for half in range(2)]
        flat = jnp.concatenate(parts, axis=0).astype(jnp.bfloat16)
        total = lax.dot_general(band, flat, (((1,), (1,)), ((), ())),
                                preferred_element_type=jnp.float32).astype(jnp.bfloat16)
        rows = pl.ds(pl.multiple_of(s * nchan, nchan), nchan)
        flat_ref[rows, pl.ds(pl.multiple_of(b * FB, FB), FB)] = total[:, 0:FB]
        flat_ref[rows, pl.ds(pl.multiple_of((nblk + b) * FB, FB), FB)] = total[:, FB:]

    load_first.wait()

    def prepare_first(k, carry):
        prepare(first, k)
        return carry

    lax.fori_loop(0, per, prepare_first, 0, unroll=True)

    @pl.when(me == 0)
    def _():
        halo[0] = jnp.zeros(halo.shape[1:], halo.dtype)
        halo_valid[0] = jnp.zeros(halo_valid.shape[1:], halo_valid.dtype)

    @pl.when(me == size - 1)
    def _():
        halo[1] = jnp.zeros(halo.shape[1:], halo.dtype)
        halo_valid[1] = jnp.zeros(halo_valid.shape[1:], halo_valid.dtype)

    def clear():
        def some(f, carry):
            cross_t[pl.ds(pl.multiple_of(f * 8 * cpitch, 8), 8 * cpitch)] = jnp.zeros((8 * cpitch, FB), jnp.float32)
            return carry

        lax.fori_loop(0, 2 * FB // 8, some, 0)
        for slot in range(nblk):
            for c in range(nchan + 2 * HALO, nrow):
                chan_t[pl.ds((slot * nrow + c) * pitch, pitch)] = jnp.zeros((pitch, depth), jnp.float32)

    def step(t, p):
        @pl.when(t == loaded)
        def _():
            for b in range(nblk):
                load(b).wait()

        @pl.when(t == loaded + 1)
        def _():
            clear()
            from_neighbours()

        for b in range(nblk):
            @pl.when(t == settled + per * (b + 1) - EARLY)
            def _():
                to_neighbours(lambda copy: copy.start(), [b])

        guarded(t, True, functools.partial(enter, t, p))
        for q in range(2):
            relay_in(q, t, p)
        for q in range(2):
            odd = (p - rooted[q]) % 2
            guarded(t - rooted[q], at_root[q][odd], functools.partial(reach_root, q, t - rooted[q], odd))
        for q in range(2):
            relay_on(q, t - rooted[q], (p - rooted[q]) % 2)
        for q in range(2):
            odd = (p - summed[q]) % 2
            guarded(t - summed[q], at_root[q][odd], functools.partial(finish, q, t - summed[q], odd))
        for q in range(2):
            spread(q, t - summed[q], (p - summed[q]) % 2)
        guarded(t - spread_at, True, lambda: back(t - spread_at, core).start())
        later = t + AHEAD
        guarded(later, later >= per, lambda: prepare(spec.at[later // per], later))
        guarded(t - turn_at, True, functools.partial(turn, t - turn_at))
        for b in range(nblk):
            @pl.when(t == settled + per * (b + 1) - 1)
            def _():
                turn_edges(b)

        now = t - settled

        @pl.when((now >= 0) & (now < per))
        def _():
            back(now, 1 - core).wait_recv()
            settle(now)

        @pl.when((now >= per) & (now < n))
        def _():
            back(now, 1 - core).wait_recv()
            b, lot = now // per - 1, now % per
            for u in range(nsrc // per):
                smooth(jnp.maximum(b - 1, 0), lot * (nsrc // per) + u)
            for u in range(FB // per):
                correlate(b, lot * (FB // per) + u)
            settle(now)

    def steps(tt, carry):
        for p in range(2):
            step(2 * tt + p, p)
        return carry

    lax.fori_loop(0, (n + settled + 1) // 2, steps, 0)

    for s in range(nsrc if nblk > 1 else 0):
        smooth(nblk - 2, s)
    for f in range(FB):
        correlate(nblk - 1, f)
    for s in range(nsrc):
        smooth(nblk - 1, s)
    all_sent()
    to_neighbours(lambda copy: copy.wait_send())
    to_neighbours(lambda copy: copy.wait_send(), range(nblk))


def lag_kernel(scale, flat_ref, table_ref, out_ref):
    half = table_ref.shape[1]
    even = jnp.dot(flat_ref[:, 0:half], table_ref[0:half], preferred_element_type=jnp.float32)
    odd = jnp.dot(flat_ref[:, half:], table_ref[half:], preferred_element_type=jnp.float32)
    out_ref[:, 0:half] = (even + odd) * scale
    out_ref[:, half:] = (even - odd) * scale


def local(size, spectra, valid, sources):
    nchan, _, nwin, nbins = spectra.shape
    nsrc = sources.shape[0]
    depth, nlags = 2 * nwin, 2 * nbins
    vmem = pl.BlockSpec(memory_space=pltpu.VMEM)

    chips = size // 2
    inner = 1
    while (2 * inner) ** 2 <= chips and chips % (2 * inner) == 0:
        inner *= 2
    outer = chips // inner
    nblk = nbins // FB
    many = MANY
    n = nblk * nsrc // (2 * many)
    nrow = -(-(nchan + 2 * HALO) // 16) * 16
    pitch, cpitch = FB + 1, 2 * nsrc + 1
    chunks = lambda *lead: pltpu.VMEM(lead + (n, 2, many, nwin, FB), jnp.bfloat16)
    flat = pl.pallas_call(
        functools.partial(cross_kernel, outer, inner, nrow),
        out_shape=pltpu.VMEM((nsrc * nchan, nlags), jnp.bfloat16),
        in_specs=[pl.BlockSpec(memory_space=pltpu.SMEM), vmem, pl.BlockSpec(memory_space=pltpu.MemorySpace.HBM)],
        out_specs=vmem,
        scratch_shapes=[pltpu.VMEM((nchan, 2, nwin, FB), jnp.bfloat16),
                        pltpu.VMEM((nblk, nchan, 2, nwin, FB), jnp.bfloat16),
                        pltpu.VMEM((2, nblk, HALO, 2, nwin, FB), jnp.bfloat16),
                        pltpu.VMEM((2, 8, nwin), jnp.int32),
                        pltpu.VMEM((nchan, depth), jnp.float32),
                        pltpu.VMEM((nsrc, nwin, FB), jnp.bfloat16),
                        chunks(), chunks(), chunks(), chunks(2), chunks(2), chunks(2),
                        pltpu.VMEM((n, 2, 2, many, nwin, FB), jnp.bfloat16),
                        pltpu.VMEM((nblk * nrow * pitch, depth), jnp.float32),
                        pltpu.VMEM((2 * 2 * nsrc * pitch, depth), jnp.float32),
                        pltpu.VMEM((2 * FB * cpitch, FB), jnp.float32),
                        pltpu.SemaphoreType.DMA((1 + nblk,)),
                        pltpu.SemaphoreType.DMA((2,)), pltpu.SemaphoreType.DMA((2, n)),
                        pltpu.SemaphoreType.DMA((6, 2, 2)), pltpu.SemaphoreType.DMA((6, 2, n)),
                        pltpu.SemaphoreType.DMA((2, nblk + 1)), pltpu.SemaphoreType.DMA((2, nblk + 1))],
        compiler_params=pltpu.CompilerParams(
            collective_id=0, has_side_effects=True, vmem_limit_bytes=56 << 20),
        name="cross",
    )(sources, valid, spectra)

    rows = nsrc * nchan // 4
    lags = pl.pallas_call(
        functools.partial(lag_kernel, 1.0 / (nwin * (2 * HALO + 1.0))),
        grid=(4,),
        out_shape=jax.ShapeDtypeStruct((nsrc * nchan, nlags), jnp.float32),
        in_specs=[pl.BlockSpec((rows, nlags), lambda at: (at, 0)),
                  pl.BlockSpec((nlags, nlags // 2), lambda at: (0, 0))],
        out_specs=pl.BlockSpec((rows, nlags), lambda at: (at, 0)),
        compiler_params=pltpu.CompilerParams(vmem_limit_bytes=24 << 20),
        name="lags",
    )(flat, jnp.asarray(make_table(nbins, nlags)))
    return lags.reshape(nsrc, nchan, nlags)


def solution(mesh):
    in_specs = (P(("grp", "chan"), None, None, None), P(("grp", "chan"), None), P("grp"))
    out_specs = P("grp", "chan", None)
    return jax.shard_map(functools.partial(local, mesh.shape["chan"]), mesh=mesh,
                         in_specs=in_specs, out_specs=out_specs, check_vma=False)
```

```python
import functools

import jax
import jax.numpy as jnp
import numpy as np
from jax import lax
from jax.experimental import pallas as pl
from jax.experimental.pallas import tpu as pltpu
from jax.sharding import PartitionSpec as P

MESH = pl.DeviceIdType.MESH
HALO = 2
HALF_LAG = 6
FIRST_EDGES = 1
AHEAD = 2
PIECES = 8
SETTLE = 2
EARLY = 5
FB = 128
MANY = 2
IN_UP, IN_DOWN, ON_UP, ON_DOWN, OUT_UP, OUT_DOWN = range(6)


def make_table(nbins, nlags):
    freq = np.arange(nbins, dtype=np.int64)
    phase = (freq[:, None] * np.arange(nlags, dtype=np.int64)[None, :]) % nlags
    angle = 2.0 * np.pi * phase / nlags
    weight = np.where(freq == 0, 1.0, 2.0) / nlags
    table = np.concatenate([weight[:, None] * np.cos(angle), -weight[:, None] * np.sin(angle)])
    order = np.concatenate([blk * FB + half * nbins + np.arange(odd, FB, 2)
                            for odd in range(2) for blk in range(nbins // FB) for half in range(2)])
    return table[order, :nlags // 2].astype(np.float32).astype(jnp.bfloat16)


def cross_kernel(outer, inner, nrow, src_hbm, valid_hbm, spec_ref, flat_ref, src_ref, valid_ref,
                 first, spec, halo, halo_valid, flags, plane, give, own, part, inward, along, passed, gathered,
                 chan_t, src_t, cross_t, load_sem, pair_send, pair_recv, send_sem, recv_sem, edge_send, edge_recv):
    nblk, nchan, _, nwin, _ = spec.shape
    nsrc, depth = plane.shape[0], 2 * nwin
    n, _, many, _, _ = give.shape
    per = n // nblk
    size = outer * inner * 2
    me = lax.axis_index("chan")
    core, chip = me % 2, me // 2
    j, i = chip % inner, chip // inner
    line_j, line_i = (j, inner, 2), (i, outer, 2 * inner)
    teeth, spine = (line_j, line_i), (line_i, line_j)
    partner = me + 1 - 2 * core
    pitch, cpitch = FB + 1, 2 * nsrc + 1

    def root(q, odd):
        length = teeth[q][1]
        return 0 if length == 1 else (length - 1) // 2 + odd

    reach = [max(root(q, 1), teeth[q][1] - 1 - root(q, 0)) for q in range(2)]
    rooted = reach
    summed = [rooted[q] + spine[q][1] - 1 for q in range(2)]

    def lag(hops):
        return (HALF_LAG * hops + 1) // 2

    spread_at = max(lag(summed[q] + reach[q]) for q in range(2))
    settled = spread_at + SETTLE
    loaded = max(per - AHEAD, 0)
    turn_at = min(loaded + 1, settled)
    at_root = [[teeth[q][0] == root(q, odd) for odd in range(2)] for q in range(2)]

    def load(b):
        return pltpu.make_async_copy(spec_ref.at[:, :, :, pl.ds(b * FB, FB)], spec.at[b], load_sem.at[1 + b])

    small = [pltpu.make_async_copy(src_hbm, src_ref, load_sem.at[1 + nblk]),
             pltpu.make_async_copy(valid_hbm, valid_ref, load_sem.at[2 + nblk])]
    for copy in small:
        copy.start()
    load_first = pltpu.make_async_copy(spec_ref.at[:, :, :, pl.ds(0, FB)], first, load_sem.at[0])
    load_first.start()
    for b in range(nblk):
        load(b).start()

    barrier = pltpu.get_barrier_semaphore()

    def greet(there):
        pl.semaphore_signal(barrier, inc=1, device_id={"chan": there}, device_id_type=MESH)

    greet(partner)
    count = jnp.int32(1)
    for pos, length, stride in (line_j, line_i, (me, size, 1)):
        @pl.when(pos > 0)
        def _():
            greet(me - stride)

        @pl.when(pos < length - 1)
        def _():
            greet(me + stride)

        count = count + (pos > 0).astype(jnp.int32) + (pos < length - 1).astype(jnp.int32)

    for copy in small:
        copy.wait()
    raw = valid_ref[...].astype(jnp.float32)
    flags[...] = jnp.concatenate([raw, raw], axis=1)
    by_window = jnp.transpose(flags[...])[0:nwin].astype(jnp.bfloat16)
    place = lax.broadcasted_iota(jnp.int32, (nchan, FB), 0)
    for s in range(nsrc):
        hot = (place == src_ref[s] - me * nchan).astype(jnp.bfloat16)
        plane[s] = jnp.dot(by_window, hot, preferred_element_type=jnp.float32).astype(jnp.bfloat16)

    pl.semaphore_wait(barrier, count)

    def edge_flags(up):
        side, eight = (0, nchan - 8) if up else (1, 0)
        return pltpu.make_async_remote_copy(
            src_ref=valid_ref.at[pl.ds(eight, 8)], dst_ref=halo_valid.at[side],
            send_sem=edge_send.at[side, nblk], recv_sem=edge_recv.at[side, nblk],
            device_id={"chan": me + 1 if up else me - 1}, device_id_type=MESH)

    def edge(up, b):
        side, rows = (0, nchan - HALO) if up else (1, 0)
        return pltpu.make_async_remote_copy(
            src_ref=spec_ref.at[pl.ds(rows, HALO), :, :, pl.ds(b * FB, FB)], dst_ref=halo.at[side, b],
            send_sem=edge_send.at[side, b], recv_sem=edge_recv.at[side, b],
            device_id={"chan": me + 1 if up else me - 1}, device_id_type=MESH)

    def to_neighbours(act, blocks=()):
        @pl.when(me < size - 1)
        def _():
            for copy in [edge(True, b) for b in blocks] or [edge_flags(True)]:
                act(copy)

        @pl.when(me > 0)
        def _():
            for copy in [edge(False, b) for b in blocks] or [edge_flags(False)]:
                act(copy)

    def from_neighbours(blocks=()):
        @pl.when(me > 0)
        def _():
            for copy in [edge(True, b) for b in blocks] or [edge_flags(True)]:
                copy.wait_recv()

        @pl.when(me < size - 1)
        def _():
            for copy in [edge(False, b) for b in blocks] or [edge_flags(False)]:
                copy.wait_recv()

    to_neighbours(lambda copy: copy.start())
    if FIRST_EDGES:
        to_neighbours(lambda copy: copy.start(), range(FIRST_EDGES))

    def across(k):
        return pltpu.make_async_remote_copy(
            src_ref=give.at[k], dst_ref=part.at[k], send_sem=pair_send.at[0], recv_sem=pair_recv.at[0, k],
            device_id={"chan": partner}, device_id_type=MESH)

    def back(k, half):
        return pltpu.make_async_remote_copy(
            src_ref=gathered.at[k, half], dst_ref=gathered.at[k, half], send_sem=pair_send.at[1],
            recv_sem=pair_recv.at[1, k], device_id={"chan": partner}, device_id_type=MESH)

    def remote(src, dst, kind, q, odd, k, there):
        return pltpu.make_async_remote_copy(
            src_ref=src, dst_ref=dst, send_sem=send_sem.at[kind, q, odd], recv_sem=recv_sem.at[kind, q, k],
            device_id={"chan": there}, device_id_type=MESH)

    def toward(q, up, odd, k):
        there = me + teeth[q][2] if up else me - teeth[q][2]
        return remote(own.at[k, q], inward.at[0 if up else 1, k, q], IN_UP if up else IN_DOWN, q, odd, k, there)

    def onward(q, up, odd, k, src):
        there = me + spine[q][2] if up else me - spine[q][2]
        return remote(src, along.at[0 if up else 1, k, q], ON_UP if up else ON_DOWN, q, odd, k, there)

    def outward(q, up, odd, k):
        there = me + teeth[q][2] if up else me - teeth[q][2]
        block = gathered.at[k, core, q]
        return remote(block, block, OUT_UP if up else OUT_DOWN, q, odd, k, there)

    def prepare(block, k):
        for q in range(2):
            for m in range(many):
                s = ((k % per) * 2 + q) * many + m
                held = jnp.clip(src_ref[s] - me * nchan, 0, nchan - 1)
                mask = plane[s]
                give[k, q, m] = block[held, 1 - core] * mask
                own[k, q, m] = block[held, core] * mask
        across(k).start()

    def guarded(k, also, run):
        @pl.when((k >= 0) & (k < n) & also)
        def _():
            run()

    def enter(k, odd):
        across(k).wait_recv()
        own[k] = own[k] + part[k]
        for q in range(2):
            pos, length, _ = teeth[q]
            if root(q, odd) > 0:
                @pl.when(pos == 0)
                def _():
                    toward(q, True, odd, k).start()

            if root(q, odd) < length - 1:
                @pl.when(pos == length - 1)
                def _():
                    toward(q, False, odd, k).start()

    def relay_in(q, t, p):
        pos, length, _ = teeth[q]
        for up in (True, False):
            for here in range(1, length - 1):
                steps = here if up else length - 1 - here
                odd = (p - lag(steps)) % 2
                k = t - lag(steps)
                if (here < root(q, odd)) if up else (here > root(q, odd)):
                    def run():
                        toward(q, up, odd, k).wait_recv()
                        own[k, q] = own[k, q] + inward[0 if up else 1, k, q]
                        toward(q, up, odd, k).start()

                    guarded(k, pos == here, run)

    def reach_root(q, k, odd):
        length = teeth[q][1]
        at, span, _ = spine[q]
        ways = []
        if root(q, odd) > 0:
            ways.append(0)
        if root(q, odd) < length - 1:
            ways.append(1)
        for way in ways:
            toward(q, way == 0, odd, k).wait_recv()
        if ways:
            total = own[k, q]
            for way in ways:
                total = total + inward[way, k, q]
            own[k, q] = total
        if span > 1:
            @pl.when(at == 0)
            def _():
                onward(q, True, odd, k, own.at[k, q]).start()

            @pl.when(at == span - 1)
            def _():
                onward(q, False, odd, k, own.at[k, q]).start()

    def relay_on(q, t, p):
        at, span, _ = spine[q]
        for up in (True, False):
            for here in range(1, span - 1):
                steps = here if up else span - 1 - here
                odd = (p - lag(rooted[q] + steps)) % 2
                k = t - lag(rooted[q] + steps)

                def run():
                    way = 0 if up else 1
                    onward(q, up, odd, k, own.at[k, q]).wait_recv()
                    passed[way, k, q] = own[k, q] + along[way, k, q]
                    onward(q, up, odd, k, passed.at[way, k, q]).start()

                guarded(k, at_root[q][odd] & (at == here), run)

    def finish(q, k, odd):
        pos, length, _ = teeth[q]
        at, span, _ = spine[q]
        if span == 1:
            gathered[k, core, q] = own[k, q]
        else:
            @pl.when(at == 0)
            def _():
                onward(q, False, odd, k, own.at[k, q]).wait_recv()
                gathered[k, core, q] = own[k, q] + along[1, k, q]

            @pl.when(at == span - 1)
            def _():
                onward(q, True, odd, k, own.at[k, q]).wait_recv()
                gathered[k, core, q] = own[k, q] + along[0, k, q]

            if span > 2:
                @pl.when((at > 0) & (at < span - 1))
                def _():
                    gathered[k, core, q] = own[k, q] + along[0, k, q] + along[1, k, q]
        if root(q, odd) < length - 1:
            outward(q, True, odd, k).start()
        if root(q, odd) > 0:
            outward(q, False, odd, k).start()

    def spread(q, t, p):
        pos, length, _ = teeth[q]
        for far in range(reach[q], 0, -1):
            odd = (p - lag(summed[q] + far)) % 2
            k = t - lag(summed[q] + far)
            for up in (True, False):
                here = root(q, odd) + far if up else root(q, odd) - far
                if 0 <= here < length:
                    def run():
                        outward(q, up, odd, k).wait_recv()
                        if (here < length - 1) if up else (here > 0):
                            outward(q, up, odd, k).start()

                    guarded(k, pos == here, run)

    def all_sent():
        def drain(block, sem):
            pltpu.make_async_remote_copy(
                src_ref=block, dst_ref=block, send_sem=sem, recv_sem=pair_recv.at[0, 0],
                device_id={"chan": partner}, device_id_type=MESH).wait_send()

        drain(give, pair_send.at[0])
        drain(give, pair_send.at[1])
        for q in range(2):
            pos, length, _ = teeth[q]
            at, span, _ = spine[q]
            for odd in range(2):
                r = root(q, odd)
                for kind, when in ((IN_UP, pos < r), (IN_DOWN, pos > r),
                                   (ON_UP, (pos == r) & (at < span - 1)), (ON_DOWN, (pos == r) & (at > 0)),
                                   (OUT_UP, (pos >= r) & (pos < length - 1)), (OUT_DOWN, (pos <= r) & (pos > 0))):
                    @pl.when(when)
                    def _():
                        drain(own.at[pl.ds(0, n // 2), q], send_sem.at[kind, q, odd])

    sign = jnp.where(lax.broadcasted_iota(jnp.int32, (1, depth), 1) < nwin, -1.0, 1.0)

    def settle(k):
        base = ((k // per) % 2) * (2 * nsrc * pitch)
        for q in range(2):
            for m in range(many):
                both = jnp.concatenate([gathered[k, 0, q, m], gathered[k, 1, q, m]], axis=0)
                x = jnp.transpose(both).astype(jnp.float32)
                s = ((k % per) * 2 + q) * many + m
                src_t[pl.ds(base + s * pitch, FB)] = x
                src_t[pl.ds(base + (s + nsrc) * pitch, FB)] = pltpu.roll(x, nwin, axis=1) * sign

    def turn(k):
        b, lot = k // per, k % per
        base = b * (nrow * pitch)
        count = nchan // per
        for u in range(count):
            c = lot * count + u
            x = jnp.transpose(spec[b, c].reshape(depth, FB)).astype(jnp.float32) * flags[pl.ds(c, 1)]
            chan_t[pl.ds(base + (c + HALO) * pitch, FB)] = x

    def turn_edges(b):
        from_neighbours([b])
        base = b * (nrow * pitch)
        for h in range(2 * HALO):
            side, c = h // HALO, h % HALO
            row = halo_valid[side][(8 - HALO + c) if side == 0 else c][None].astype(jnp.float32)
            row = jnp.concatenate([row, row], axis=1)
            x = jnp.transpose(halo[side, b, c].reshape(depth, FB)).astype(jnp.float32) * row
            chan_t[pl.ds(base + (c + side * (HALO + nchan)) * pitch, FB)] = x

    def correlate(b, f):
        right = chan_t[pl.ds(b * (nrow * pitch) + f, nrow, stride=pitch)].astype(jnp.bfloat16)
        left = src_t[pl.ds((b % 2) * (2 * nsrc * pitch) + f, 2 * nsrc, stride=pitch)].astype(jnp.bfloat16)
        both = lax.dot_general(left, right, (((1,), (1,)), ((), ())), preferred_element_type=jnp.float32)
        cross_t[pl.ds((b % 2) * (FB * cpitch) + f * cpitch, 2 * nsrc), 0:nrow] = both

    ahead = (lax.broadcasted_iota(jnp.int32, (nchan, FB), 1)
             - lax.broadcasted_iota(jnp.int32, (nchan, FB), 0))
    band = ((ahead >= 0) & (ahead <= 2 * HALO)).astype(jnp.bfloat16)

    def smooth(b, s):
        base = (b % 2) * (FB * cpitch)
        parts = [cross_t[pl.ds(base + odd * cpitch + s + half * nsrc, FB // 2, stride=2 * cpitch)]
                 for odd in range(2) for half in range(2)]
        flat = jnp.concatenate(parts, axis=0).astype(jnp.bfloat16)
        total = lax.dot_general(band, flat, (((1,), (1,)), ((), ())),
                                preferred_element_type=jnp.float32).astype(jnp.bfloat16)
        rows = pl.ds(pl.multiple_of(s * nchan, nchan), nchan)
        flat_ref[rows, pl.ds(pl.multiple_of(b * FB, FB), FB)] = total[:, 0:FB]
        flat_ref[rows, pl.ds(pl.multiple_of((nblk + b) * FB, FB), FB)] = total[:, FB:]

    load_first.wait()

    def prepare_first(k, carry):
        prepare(first, k)
        return carry

    lax.fori_loop(0, per, prepare_first, 0, unroll=True)

    @pl.when(me == 0)
    def _():
        halo[0] = jnp.zeros(halo.shape[1:], halo.dtype)
        halo_valid[0] = jnp.zeros(halo_valid.shape[1:], halo_valid.dtype)

    @pl.when(me == size - 1)
    def _():
        halo[1] = jnp.zeros(halo.shape[1:], halo.dtype)
        halo_valid[1] = jnp.zeros(halo_valid.shape[1:], halo_valid.dtype)

    def clear():
        def some(f, carry):
            cross_t[pl.ds(pl.multiple_of(f * 8 * cpitch, 8), 8 * cpitch)] = jnp.zeros((8 * cpitch, FB), jnp.float32)
            return carry

        lax.fori_loop(0, 2 * FB // 8, some, 0)
        for slot in range(nblk):
            for c in range(nchan + 2 * HALO, nrow):
                chan_t[pl.ds((slot * nrow + c) * pitch, pitch)] = jnp.zeros((pitch, depth), jnp.float32)

    def step(t, p):
        @pl.when(t == loaded)
        def _():
            for b in range(nblk):
                load(b).wait()

        @pl.when(t == loaded + 1)
        def _():
            clear()
            from_neighbours()

        for b in range(FIRST_EDGES, nblk):
            @pl.when(t == settled + per * (b + 1) - EARLY)
            def _():
                to_neighbours(lambda copy: copy.start(), [b])

        guarded(t, True, functools.partial(enter, t, p))
        for q in range(2):
            relay_in(q, t, p)
        for q in range(2):
            at = lag(rooted[q])
            odd = (p - at) % 2
            guarded(t - at, at_root[q][odd], functools.partial(reach_root, q, t - at, odd))
        for q in range(2):
            relay_on(q, t, p)
        for q in range(2):
            at = lag(summed[q])
            odd = (p - at) % 2
            guarded(t - at, at_root[q][odd], functools.partial(finish, q, t - at, odd))
        for q in range(2):
            spread(q, t, p)
        guarded(t - spread_at, True, lambda: back(t - spread_at, core).start())
        later = t + AHEAD
        guarded(later, later >= per, lambda: prepare(spec.at[later // per], later))
        guarded(t - turn_at, True, functools.partial(turn, t - turn_at))
        for b in range(nblk):
            @pl.when(t == settled + per * (b + 1) - 1)
            def _():
                turn_edges(b)

        now = t - settled

        @pl.when((now >= 0) & (now < per))
        def _():
            back(now, 1 - core).wait_recv()
            settle(now)

        @pl.when((now >= per) & (now < n))
        def _():
            back(now, 1 - core).wait_recv()
            b, lot = now // per - 1, now % per
            for u in range(nsrc // per):
                smooth(jnp.maximum(b - 1, 0), lot * (nsrc // per) + u)
            for u in range(FB // per):
                correlate(b, lot * (FB // per) + u)
            settle(now)

    def steps(tt, carry):
        for p in range(2):
            step(2 * tt + p, p)
        return carry

    lax.fori_loop(0, (n + settled + 1) // 2, steps, 0)

    for s in range(nsrc if nblk > 1 else 0):
        smooth(nblk - 2, s)
    for f in range(FB):
        correlate(nblk - 1, f)
    for s in range(nsrc):
        smooth(nblk - 1, s)
    all_sent()
    to_neighbours(lambda copy: copy.wait_send())
    to_neighbours(lambda copy: copy.wait_send(), range(nblk))


def lag_kernel(scale, flat_ref, table_ref, out_ref, lags, sems):
    half = table_ref.shape[1]
    rows = lags.shape[1]
    copies = []
    for piece in range(PIECES):
        at = pl.ds(piece * rows, rows)
        even = jnp.dot(flat_ref[at, 0:half], table_ref[0:half], preferred_element_type=jnp.float32)
        odd = jnp.dot(flat_ref[at, half:], table_ref[half:], preferred_element_type=jnp.float32)
        lags[piece, :, 0:half] = (even + odd) * scale
        lags[piece, :, half:] = (even - odd) * scale
        copy = pltpu.make_async_copy(lags.at[piece], out_ref.at[at], sems.at[piece])
        copy.start()
        copies.append(copy)
    for copy in copies:
        copy.wait()


def local(size, spectra, valid, sources):
    nchan, _, nwin, nbins = spectra.shape
    nsrc = sources.shape[0]
    depth, nlags = 2 * nwin, 2 * nbins
    vmem = pl.BlockSpec(memory_space=pltpu.VMEM)

    chips = size // 2
    inner = 1
    while (2 * inner) ** 2 <= chips and chips % (2 * inner) == 0:
        inner *= 2
    outer = chips // inner
    nblk = nbins // FB
    many = MANY
    n = nblk * nsrc // (2 * many)
    nrow = -(-(nchan + 2 * HALO) // 16) * 16
    pitch, cpitch = FB + 1, 2 * nsrc + 1
    chunks = lambda *lead: pltpu.VMEM(lead + (n, 2, many, nwin, FB), jnp.bfloat16)
    flat = pl.pallas_call(
        functools.partial(cross_kernel, outer, inner, nrow),
        out_shape=pltpu.VMEM((nsrc * nchan, nlags), jnp.bfloat16),
        in_specs=[pl.BlockSpec(memory_space=pltpu.MemorySpace.HBM)] * 3,
        out_specs=vmem,
        scratch_shapes=[pltpu.SMEM((nsrc,), jnp.int32), pltpu.VMEM((nchan, nwin), jnp.int32),
                        pltpu.VMEM((nchan, 2, nwin, FB), jnp.bfloat16),
                        pltpu.VMEM((nblk, nchan, 2, nwin, FB), jnp.bfloat16),
                        pltpu.VMEM((2, nblk, HALO, 2, nwin, FB), jnp.bfloat16),
                        pltpu.VMEM((2, 8, nwin), jnp.int32),
                        pltpu.VMEM((nchan, depth), jnp.float32),
                        pltpu.VMEM((nsrc, nwin, FB), jnp.bfloat16),
                        chunks(), chunks(), chunks(), chunks(2), chunks(2), chunks(2),
                        pltpu.VMEM((n, 2, 2, many, nwin, FB), jnp.bfloat16),
                        pltpu.VMEM((nblk * nrow * pitch, depth), jnp.float32),
                        pltpu.VMEM((2 * 2 * nsrc * pitch, depth), jnp.float32),
                        pltpu.VMEM((2 * FB * cpitch, FB), jnp.float32),
                        pltpu.SemaphoreType.DMA((3 + nblk,)),
                        pltpu.SemaphoreType.DMA((2,)), pltpu.SemaphoreType.DMA((2, n)),
                        pltpu.SemaphoreType.DMA((6, 2, 2)), pltpu.SemaphoreType.DMA((6, 2, n)),
                        pltpu.SemaphoreType.DMA((2, nblk + 1)), pltpu.SemaphoreType.DMA((2, nblk + 1))],
        compiler_params=pltpu.CompilerParams(
            collective_id=0, has_side_effects=True, vmem_limit_bytes=56 << 20),
        name="cross",
    )(sources, valid, spectra)

    rows = nsrc * nchan // PIECES
    lags = pl.pallas_call(
        functools.partial(lag_kernel, 1.0 / (nwin * (2 * HALO + 1.0))),
        out_shape=jax.ShapeDtypeStruct((nsrc * nchan, nlags), jnp.float32),
        in_specs=[vmem, vmem],
        out_specs=pl.BlockSpec(memory_space=pltpu.MemorySpace.HBM),
        scratch_shapes=[pltpu.VMEM((PIECES, rows, nlags), jnp.float32), pltpu.SemaphoreType.DMA((PIECES,))],
        compiler_params=pltpu.CompilerParams(vmem_limit_bytes=24 << 20),
        name="lags",
    )(flat, jnp.asarray(make_table(nbins, nlags)))
    return lags.reshape(nsrc, nchan, nlags)


def solution(mesh):
    in_specs = (P(("grp", "chan"), None, None, None), P(("grp", "chan"), None), P("grp"))
    out_specs = P("grp", "chan", None)
    return jax.shard_map(functools.partial(local, mesh.shape["chan"]), mesh=mesh,
                         in_specs=in_specs, out_specs=out_specs, check_vma=False)
```

```python
import functools

import jax
import jax.numpy as jnp
import numpy as np
from jax import lax
from jax.experimental import pallas as pl
from jax.experimental.pallas import tpu as pltpu
from jax.sharding import PartitionSpec as P

MESH = pl.DeviceIdType.MESH
HALO = 2
HALF_LAG = 6
FIRST_EDGES = 1
AHEAD = 2
PIECES = 8
SETTLE = 2
EARLY = 5
FB = 128
MANY = 2
IN_UP, IN_DOWN, ON_UP, ON_DOWN, OUT_UP, OUT_DOWN = range(6)


def make_table(nbins, nlags):
    freq = np.arange(nbins, dtype=np.int64)
    phase = (freq[:, None] * np.arange(nlags, dtype=np.int64)[None, :]) % nlags
    angle = 2.0 * np.pi * phase / nlags
    weight = np.where(freq == 0, 1.0, 2.0) / nlags
    table = np.concatenate([weight[:, None] * np.cos(angle), -weight[:, None] * np.sin(angle)])
    order = np.concatenate([blk * FB + half * nbins + np.arange(odd, FB, 2)
                            for odd in range(2) for blk in range(nbins // FB) for half in range(2)])
    return table[order, :nlags // 2].astype(np.float32).astype(jnp.bfloat16)


def cross_kernel(outer, inner, nrow, src_hbm, valid_hbm, spec_ref, flat_ref, src_ref, valid_ref,
                 first, spec, halo, halo_valid, flags, plane, give, own, part, inward, along, passed, gathered,
                 chan_t, src_t, cross_t, load_sem, pair_send, pair_recv, send_sem, recv_sem, edge_send, edge_recv):
    nblk, nchan, _, nwin, _ = spec.shape
    nsrc, depth = plane.shape[0], 2 * nwin
    n, _, many, _, _ = give.shape
    per = n // nblk
    size = outer * inner * 2
    me = lax.axis_index("chan")
    core, chip = me % 2, me // 2
    j, i = chip % inner, chip // inner
    line_j, line_i = (j, inner, 2), (i, outer, 2 * inner)
    teeth, spine = (line_j, line_i), (line_i, line_j)
    partner = me + 1 - 2 * core
    pitch, cpitch = FB + 1, 2 * nsrc + 1

    def root(q, odd):
        length = teeth[q][1]
        return 0 if length == 1 else (length - 1) // 2 + odd

    reach = [max(root(q, 1), teeth[q][1] - 1 - root(q, 0)) for q in range(2)]
    rooted = reach
    summed = [rooted[q] + spine[q][1] - 1 for q in range(2)]

    def lag(hops):
        return (HALF_LAG * hops + 1) // 2

    spread_at = max(lag(summed[q] + reach[q]) for q in range(2))
    settled = spread_at + SETTLE
    loaded = max(per - AHEAD, 0)
    turn_at = min(loaded + 1, settled)
    at_root = [[teeth[q][0] == root(q, odd) for odd in range(2)] for q in range(2)]

    def load(b):
        return pltpu.make_async_copy(spec_ref.at[:, :, :, pl.ds(b * FB, FB)], spec.at[b], load_sem.at[1 + b])

    small = [pltpu.make_async_copy(src_hbm, src_ref, load_sem.at[1 + nblk]),
             pltpu.make_async_copy(valid_hbm, valid_ref, load_sem.at[2 + nblk])]
    for copy in small:
        copy.start()
    load_first = pltpu.make_async_copy(spec_ref.at[:, :, :, pl.ds(0, FB)], first, load_sem.at[0])
    load_first.start()
    for b in range(nblk):
        load(b).start()

    barrier = pltpu.get_barrier_semaphore()

    def greet(there):
        pl.semaphore_signal(barrier, inc=1, device_id={"chan": there}, device_id_type=MESH)

    greet(partner)
    count = jnp.int32(1)
    for pos, length, stride in (line_j, line_i, (me, size, 1)):
        @pl.when(pos > 0)
        def _():
            greet(me - stride)

        @pl.when(pos < length - 1)
        def _():
            greet(me + stride)

        count = count + (pos > 0).astype(jnp.int32) + (pos < length - 1).astype(jnp.int32)

    for copy in small:
        copy.wait()
    raw = valid_ref[...].astype(jnp.float32)
    flags[...] = jnp.concatenate([raw, raw], axis=1)
    by_window = jnp.transpose(flags[...])[0:nwin].astype(jnp.bfloat16)
    place = lax.broadcasted_iota(jnp.int32, (nchan, FB), 0)
    for s in range(nsrc):
        hot = (place == src_ref[s] - me * nchan).astype(jnp.bfloat16)
        plane[s] = jnp.dot(by_window, hot, preferred_element_type=jnp.float32).astype(jnp.bfloat16)

    pl.semaphore_wait(barrier, count)

    def edge_flags(up):
        side, eight = (0, nchan - 8) if up else (1, 0)
        return pltpu.make_async_remote_copy(
            src_ref=valid_ref.at[pl.ds(eight, 8)], dst_ref=halo_valid.at[side],
            send_sem=edge_send.at[side, nblk], recv_sem=edge_recv.at[side, nblk],
            device_id={"chan": me + 1 if up else me - 1}, device_id_type=MESH)

    def edge(up, b):
        side, rows = (0, nchan - HALO) if up else (1, 0)
        return pltpu.make_async_remote_copy(
            src_ref=spec_ref.at[pl.ds(rows, HALO), :, :, pl.ds(b * FB, FB)], dst_ref=halo.at[side, b],
            send_sem=edge_send.at[side, b], recv_sem=edge_recv.at[side, b],
            device_id={"chan": me + 1 if up else me - 1}, device_id_type=MESH)

    def to_neighbours(act, blocks=()):
        @pl.when(me < size - 1)
        def _():
            for copy in [edge(True, b) for b in blocks] or [edge_flags(True)]:
                act(copy)

        @pl.when(me > 0)
        def _():
            for copy in [edge(False, b) for b in blocks] or [edge_flags(False)]:
                act(copy)

    def from_neighbours(blocks=()):
        @pl.when(me > 0)
        def _():
            for copy in [edge(True, b) for b in blocks] or [edge_flags(True)]:
                copy.wait_recv()

        @pl.when(me < size - 1)
        def _():
            for copy in [edge(False, b) for b in blocks] or [edge_flags(False)]:
                copy.wait_recv()

    to_neighbours(lambda copy: copy.start())
    if FIRST_EDGES:
        to_neighbours(lambda copy: copy.start(), range(FIRST_EDGES))

    def across(k):
        return pltpu.make_async_remote_copy(
            src_ref=give.at[k], dst_ref=part.at[k], send_sem=pair_send.at[0], recv_sem=pair_recv.at[0, k],
            device_id={"chan": partner}, device_id_type=MESH)

    def back(k, half):
        return pltpu.make_async_remote_copy(
            src_ref=gathered.at[k, half], dst_ref=gathered.at[k, half], send_sem=pair_send.at[1],
            recv_sem=pair_recv.at[1, k], device_id={"chan": partner}, device_id_type=MESH)

    def remote(src, dst, kind, q, odd, k, there):
        return pltpu.make_async_remote_copy(
            src_ref=src, dst_ref=dst, send_sem=send_sem.at[kind, q, odd], recv_sem=recv_sem.at[kind, q, k],
            device_id={"chan": there}, device_id_type=MESH)

    def toward(q, up, odd, k):
        there = me + teeth[q][2] if up else me - teeth[q][2]
        return remote(own.at[k, q], inward.at[0 if up else 1, k, q], IN_UP if up else IN_DOWN, q, odd, k, there)

    def onward(q, up, odd, k, src):
        there = me + spine[q][2] if up else me - spine[q][2]
        return remote(src, along.at[0 if up else 1, k, q], ON_UP if up else ON_DOWN, q, odd, k, there)

    def outward(q, up, odd, k):
        there = me + teeth[q][2] if up else me - teeth[q][2]
        block = gathered.at[k, core, q]
        return remote(block, block, OUT_UP if up else OUT_DOWN, q, odd, k, there)

    def prepare(block, k):
        for q in range(2):
            for m in range(many):
                s = ((k % per) * 2 + q) * many + m
                held = jnp.clip(src_ref[s] - me * nchan, 0, nchan - 1)
                mask = plane[s]
                give[k, q, m] = block[held, 1 - core] * mask
                own[k, q, m] = block[held, core] * mask
        across(k).start()

    def guarded(k, also, run):
        @pl.when((k >= 0) & (k < n) & also)
        def _():
            run()

    def enter(k, odd):
        across(k).wait_recv()
        own[k] = own[k] + part[k]
        for q in range(2):
            pos, length, _ = teeth[q]
            if root(q, odd) > 0:
                @pl.when(pos == 0)
                def _():
                    toward(q, True, odd, k).start()

            if root(q, odd) < length - 1:
                @pl.when(pos == length - 1)
                def _():
                    toward(q, False, odd, k).start()

    def relay_in(q, t, p):
        pos, length, _ = teeth[q]
        for up in (True, False):
            for here in range(1, length - 1):
                steps = here if up else length - 1 - here
                odd = (p - lag(steps)) % 2
                k = t - lag(steps)
                if (here < root(q, odd)) if up else (here > root(q, odd)):
                    def run():
                        toward(q, up, odd, k).wait_recv()
                        own[k, q] = own[k, q] + inward[0 if up else 1, k, q]
                        toward(q, up, odd, k).start()

                    guarded(k, pos == here, run)

    def reach_root(q, k, odd):
        length = teeth[q][1]
        at, span, _ = spine[q]
        ways = []
        if root(q, odd) > 0:
            ways.append(0)
        if root(q, odd) < length - 1:
            ways.append(1)
        for way in ways:
            toward(q, way == 0, odd, k).wait_recv()
        if ways:
            total = own[k, q]
            for way in ways:
                total = total + inward[way, k, q]
            own[k, q] = total
        if span > 1:
            @pl.when(at == 0)
            def _():
                onward(q, True, odd, k, own.at[k, q]).start()

            @pl.when(at == span - 1)
            def _():
                onward(q, False, odd, k, own.at[k, q]).start()

    def relay_on(q, t, p):
        at, span, _ = spine[q]
        for up in (True, False):
            for here in range(1, span - 1):
                steps = here if up else span - 1 - here
                odd = (p - lag(rooted[q] + steps)) % 2
                k = t - lag(rooted[q] + steps)

                def run():
                    way = 0 if up else 1
                    onward(q, up, odd, k, own.at[k, q]).wait_recv()
                    passed[way, k, q] = own[k, q] + along[way, k, q]
                    onward(q, up, odd, k, passed.at[way, k, q]).start()

                guarded(k, at_root[q][odd] & (at == here), run)

    def finish(q, k, odd):
        pos, length, _ = teeth[q]
        at, span, _ = spine[q]
        if span == 1:
            gathered[k, core, q] = own[k, q]
        else:
            @pl.when(at == 0)
            def _():
                onward(q, False, odd, k, own.at[k, q]).wait_recv()
                gathered[k, core, q] = own[k, q] + along[1, k, q]

            @pl.when(at == span - 1)
            def _():
                onward(q, True, odd, k, own.at[k, q]).wait_recv()
                gathered[k, core, q] = own[k, q] + along[0, k, q]

            if span > 2:
                @pl.when((at > 0) & (at < span - 1))
                def _():
                    gathered[k, core, q] = own[k, q] + along[0, k, q] + along[1, k, q]
        if root(q, odd) < length - 1:
            outward(q, True, odd, k).start()
        if root(q, odd) > 0:
            outward(q, False, odd, k).start()

    def spread(q, t, p):
        pos, length, _ = teeth[q]
        for far in range(reach[q], 0, -1):
            odd = (p - lag(summed[q] + far)) % 2
            k = t - lag(summed[q] + far)
            for up in (True, False):
                here = root(q, odd) + far if up else root(q, odd) - far
                if 0 <= here < length:
                    def run():
                        outward(q, up, odd, k).wait_recv()
                        if (here < length - 1) if up else (here > 0):
                            outward(q, up, odd, k).start()

                    guarded(k, pos == here, run)

    def all_sent():
        def drain(block, sem):
            pltpu.make_async_remote_copy(
                src_ref=block, dst_ref=block, send_sem=sem, recv_sem=pair_recv.at[0, 0],
                device_id={"chan": partner}, device_id_type=MESH).wait_send()

        drain(give, pair_send.at[0])
        drain(give, pair_send.at[1])
        for q in range(2):
            pos, length, _ = teeth[q]
            at, span, _ = spine[q]
            for odd in range(2):
                r = root(q, odd)
                for kind, when in ((IN_UP, pos < r), (IN_DOWN, pos > r),
                                   (ON_UP, (pos == r) & (at < span - 1)), (ON_DOWN, (pos == r) & (at > 0)),
                                   (OUT_UP, (pos >= r) & (pos < length - 1)), (OUT_DOWN, (pos <= r) & (pos > 0))):
                    @pl.when(when)
                    def _():
                        drain(own.at[pl.ds(0, n // 2), q], send_sem.at[kind, q, odd])

    sign = jnp.where(lax.broadcasted_iota(jnp.int32, (1, depth), 1) < nwin, -1.0, 1.0)

    def settle(k):
        base = ((k // per) % 2) * (2 * nsrc * pitch)
        for q in range(2):
            for m in range(many):
                both = jnp.concatenate([gathered[k, 0, q, m], gathered[k, 1, q, m]], axis=0)
                x = jnp.transpose(both).astype(jnp.float32)
                s = ((k % per) * 2 + q) * many + m
                src_t[pl.ds(base + s * pitch, FB)] = x
                src_t[pl.ds(base + (s + nsrc) * pitch, FB)] = pltpu.roll(x, nwin, axis=1) * sign

    def turn(k):
        b, lot = k // per, k % per
        base = b * (nrow * pitch)
        count = nchan // per
        for u in range(count):
            c = lot * count + u
            x = jnp.transpose(spec[b, c].reshape(depth, FB)).astype(jnp.float32) * flags[pl.ds(c, 1)]
            chan_t[pl.ds(base + (c + HALO) * pitch, FB)] = x

    def turn_edges(b):
        from_neighbours([b])
        base = b * (nrow * pitch)
        for h in range(2 * HALO):
            side, c = h // HALO, h % HALO
            row = halo_valid[side][(8 - HALO + c) if side == 0 else c][None].astype(jnp.float32)
            row = jnp.concatenate([row, row], axis=1)
            x = jnp.transpose(halo[side, b, c].reshape(depth, FB)).astype(jnp.float32) * row
            chan_t[pl.ds(base + (c + side * (HALO + nchan)) * pitch, FB)] = x

    nothing = jnp.zeros((2 * nsrc, depth), jnp.bfloat16)

    def correlate(b, f):
        def rows(ref, base, count, at):
            return ref[pl.ds(base + at, count, stride=pitch)].astype(jnp.bfloat16)

        right = [rows(chan_t, b * (nrow * pitch), nrow, f + u) for u in range(2)]
        left = [rows(src_t, (b % 2) * (2 * nsrc * pitch), 2 * nsrc, f + u) for u in range(2)]
        left = jnp.concatenate([jnp.concatenate([left[0], nothing], axis=1),
                                jnp.concatenate([nothing, left[1]], axis=1)], axis=0)
        both = lax.dot_general(left, jnp.concatenate(right, axis=1), (((1,), (1,)), ((), ())),
                               preferred_element_type=jnp.float32)
        for u in range(2):
            at = (b % 2) * (FB * cpitch) + (f + u) * cpitch
            cross_t[pl.ds(at, 2 * nsrc), 0:nrow] = both[2 * nsrc * u:2 * nsrc * (u + 1)]

    ahead = (lax.broadcasted_iota(jnp.int32, (nchan, FB), 1)
             - lax.broadcasted_iota(jnp.int32, (nchan, FB), 0))
    band = ((ahead >= 0) & (ahead <= 2 * HALO)).astype(jnp.bfloat16)
    apart = jnp.zeros_like(band)
    bands = jnp.concatenate([jnp.concatenate([band, apart], axis=1),
                             jnp.concatenate([apart, band], axis=1)], axis=0)

    def smooth(b, s):
        base = (b % 2) * (FB * cpitch)
        flats = []
        for u in range(2):
            parts = [cross_t[pl.ds(base + odd * cpitch + s + u + half * nsrc, FB // 2, stride=2 * cpitch)]
                     for odd in range(2) for half in range(2)]
            flats.append(jnp.concatenate(parts, axis=0).astype(jnp.bfloat16))
        total = lax.dot_general(bands, jnp.concatenate(flats, axis=1), (((1,), (1,)), ((), ())),
                                preferred_element_type=jnp.float32).astype(jnp.bfloat16)
        rows = pl.ds(pl.multiple_of(s * nchan, nchan), 2 * nchan)
        flat_ref[rows, pl.ds(pl.multiple_of(b * FB, FB), FB)] = total[:, 0:FB]
        flat_ref[rows, pl.ds(pl.multiple_of((nblk + b) * FB, FB), FB)] = total[:, FB:]

    load_first.wait()

    def prepare_first(k, carry):
        prepare(first, k)
        return carry

    lax.fori_loop(0, per, prepare_first, 0, unroll=True)

    @pl.when(me == 0)
    def _():
        halo[0] = jnp.zeros(halo.shape[1:], halo.dtype)
        halo_valid[0] = jnp.zeros(halo_valid.shape[1:], halo_valid.dtype)

    @pl.when(me == size - 1)
    def _():
        halo[1] = jnp.zeros(halo.shape[1:], halo.dtype)
        halo_valid[1] = jnp.zeros(halo_valid.shape[1:], halo_valid.dtype)

    def clear():
        def some(f, carry):
            cross_t[pl.ds(pl.multiple_of(f * 8 * cpitch, 8), 8 * cpitch)] = jnp.zeros((8 * cpitch, FB), jnp.float32)
            return carry

        lax.fori_loop(0, 2 * FB // 8, some, 0)
        for slot in range(nblk):
            for c in range(nchan + 2 * HALO, nrow):
                chan_t[pl.ds((slot * nrow + c) * pitch, pitch)] = jnp.zeros((pitch, depth), jnp.float32)

    def step(t, p):
        @pl.when(t == loaded)
        def _():
            for b in range(nblk):
                load(b).wait()

        @pl.when(t == loaded + 1)
        def _():
            clear()
            from_neighbours()

        for b in range(FIRST_EDGES, nblk):
            @pl.when(t == settled + per * (b + 1) - EARLY)
            def _():
                to_neighbours(lambda copy: copy.start(), [b])

        guarded(t, True, functools.partial(enter, t, p))
        for q in range(2):
            relay_in(q, t, p)
        for q in range(2):
            at = lag(rooted[q])
            odd = (p - at) % 2
            guarded(t - at, at_root[q][odd], functools.partial(reach_root, q, t - at, odd))
        now = t - settled

        @pl.when((now >= 0) & (now < per))
        def _():
            back(now, 1 - core).wait_recv()
            settle(now)

        @pl.when((now >= per) & (now < n))
        def _():
            back(now, 1 - core).wait_recv()
            b, lot = now // per - 1, now % per
            for u in range(0, nsrc // per, 2):
                smooth(jnp.maximum(b - 1, 0), lot * (nsrc // per) + u)
            for u in range(0, FB // per, 2):
                correlate(b, lot * (FB // per) + u)
            settle(now)

        for q in range(2):
            relay_on(q, t, p)
        for q in range(2):
            at = lag(summed[q])
            odd = (p - at) % 2
            guarded(t - at, at_root[q][odd], functools.partial(finish, q, t - at, odd))
        for q in range(2):
            spread(q, t, p)
        guarded(t - spread_at, True, lambda: back(t - spread_at, core).start())
        later = t + AHEAD
        guarded(later, later >= per, lambda: prepare(spec.at[later // per], later))
        guarded(t - turn_at, True, functools.partial(turn, t - turn_at))
        for b in range(nblk):
            @pl.when(t == settled + per * (b + 1) - 1)
            def _():
                turn_edges(b)


    def steps(tt, carry):
        for p in range(2):
            step(2 * tt + p, p)
        return carry

    lax.fori_loop(0, (n + settled + 1) // 2, steps, 0)

    for s in range(0, nsrc if nblk > 1 else 0, 2):
        smooth(nblk - 2, s)
    for f in range(0, FB, 2):
        correlate(nblk - 1, f)
    for s in range(0, nsrc, 2):
        smooth(nblk - 1, s)
    all_sent()
    to_neighbours(lambda copy: copy.wait_send())
    to_neighbours(lambda copy: copy.wait_send(), range(nblk))


def lag_kernel(scale, flat_ref, table_ref, out_ref, lags, sems):
    half = table_ref.shape[1]
    rows = lags.shape[1]
    copies = []
    for piece in range(PIECES):
        at = pl.ds(piece * rows, rows)
        even = jnp.dot(flat_ref[at, 0:half], table_ref[0:half], preferred_element_type=jnp.float32)
        odd = jnp.dot(flat_ref[at, half:], table_ref[half:], preferred_element_type=jnp.float32)
        lags[piece, :, 0:half] = (even + odd) * scale
        lags[piece, :, half:] = (even - odd) * scale
        copy = pltpu.make_async_copy(lags.at[piece], out_ref.at[at], sems.at[piece])
        copy.start()
        copies.append(copy)
    for copy in copies:
        copy.wait()


def local(size, spectra, valid, sources):
    nchan, _, nwin, nbins = spectra.shape
    nsrc = sources.shape[0]
    depth, nlags = 2 * nwin, 2 * nbins
    vmem = pl.BlockSpec(memory_space=pltpu.VMEM)

    chips = size // 2
    inner = 1
    while (2 * inner) ** 2 <= chips and chips % (2 * inner) == 0:
        inner *= 2
    outer = chips // inner
    nblk = nbins // FB
    many = MANY
    n = nblk * nsrc // (2 * many)
    nrow = -(-(nchan + 2 * HALO) // 16) * 16
    pitch, cpitch = FB + 1, 2 * nsrc + 1
    chunks = lambda *lead: pltpu.VMEM(lead + (n, 2, many, nwin, FB), jnp.bfloat16)
    flat = pl.pallas_call(
        functools.partial(cross_kernel, outer, inner, nrow),
        out_shape=pltpu.VMEM((nsrc * nchan, nlags), jnp.bfloat16),
        in_specs=[pl.BlockSpec(memory_space=pltpu.MemorySpace.HBM)] * 3,
        out_specs=vmem,
        scratch_shapes=[pltpu.SMEM((nsrc,), jnp.int32), pltpu.VMEM((nchan, nwin), jnp.int32),
                        pltpu.VMEM((nchan, 2, nwin, FB), jnp.bfloat16),
                        pltpu.VMEM((nblk, nchan, 2, nwin, FB), jnp.bfloat16),
                        pltpu.VMEM((2, nblk, HALO, 2, nwin, FB), jnp.bfloat16),
                        pltpu.VMEM((2, 8, nwin), jnp.int32),
                        pltpu.VMEM((nchan, depth), jnp.float32),
                        pltpu.VMEM((nsrc, nwin, FB), jnp.bfloat16),
                        chunks(), chunks(), chunks(), chunks(2), chunks(2), chunks(2),
                        pltpu.VMEM((n, 2, 2, many, nwin, FB), jnp.bfloat16),
                        pltpu.VMEM((nblk * nrow * pitch, depth), jnp.float32),
                        pltpu.VMEM((2 * 2 * nsrc * pitch, depth), jnp.float32),
                        pltpu.VMEM((2 * FB * cpitch, FB), jnp.float32),
                        pltpu.SemaphoreType.DMA((3 + nblk,)),
                        pltpu.SemaphoreType.DMA((2,)), pltpu.SemaphoreType.DMA((2, n)),
                        pltpu.SemaphoreType.DMA((6, 2, 2)), pltpu.SemaphoreType.DMA((6, 2, n)),
                        pltpu.SemaphoreType.DMA((2, nblk + 1)), pltpu.SemaphoreType.DMA((2, nblk + 1))],
        compiler_params=pltpu.CompilerParams(
            collective_id=0, has_side_effects=True, vmem_limit_bytes=56 << 20),
        name="cross",
    )(sources, valid, spectra)

    rows = nsrc * nchan // PIECES
    lags = pl.pallas_call(
        functools.partial(lag_kernel, 1.0 / (nwin * (2 * HALO + 1.0))),
        out_shape=jax.ShapeDtypeStruct((nsrc * nchan, nlags), jnp.float32),
        in_specs=[vmem, vmem],
        out_specs=pl.BlockSpec(memory_space=pltpu.MemorySpace.HBM),
        scratch_shapes=[pltpu.VMEM((PIECES, rows, nlags), jnp.float32), pltpu.SemaphoreType.DMA((PIECES,))],
        compiler_params=pltpu.CompilerParams(vmem_limit_bytes=24 << 20),
        name="lags",
    )(flat, jnp.asarray(make_table(nbins, nlags)))
    return lags.reshape(nsrc, nchan, nlags)


def solution(mesh):
    in_specs = (P(("grp", "chan"), None, None, None), P(("grp", "chan"), None), P("grp"))
    out_specs = P("grp", "chan", None)
    return jax.shard_map(functools.partial(local, mesh.shape["chan"]), mesh=mesh,
                         in_specs=in_specs, out_specs=out_specs, check_vma=False)
```

```python
import functools

import jax
import jax.numpy as jnp
import numpy as np
from jax import lax
from jax.experimental import pallas as pl
from jax.experimental.pallas import tpu as pltpu
from jax.sharding import PartitionSpec as P

MESH = pl.DeviceIdType.MESH
HALO = 2
HALF_LAG = 6
FIRST_EDGES = 1
AHEAD = 2
PIECES = 8
SETTLE = 2
EARLY = 5
FB = 128
MANY = 2
IN_UP, IN_DOWN, ON_UP, ON_DOWN, OUT_UP, OUT_DOWN = range(6)


def make_table(nbins, nlags):
    freq = np.arange(nbins, dtype=np.int64)
    phase = (freq[:, None] * np.arange(nlags, dtype=np.int64)[None, :]) % nlags
    angle = 2.0 * np.pi * phase / nlags
    weight = np.where(freq == 0, 1.0, 2.0) / nlags
    table = np.concatenate([weight[:, None] * np.cos(angle), -weight[:, None] * np.sin(angle)])
    order = np.concatenate([blk * FB + half * nbins + np.arange(odd, FB, 2)
                            for odd in range(2) for blk in range(nbins // FB) for half in range(2)])
    return table[order, :nlags // 2].astype(np.float32).astype(jnp.bfloat16)


def cross_kernel(outer, inner, nrow, src_hbm, valid_hbm, spec_ref, flat_ref, src_ref, valid_ref,
                 first, spec, halo, halo_valid, flags, plane, give, own, part, inward, along, passed, gathered,
                 chan_t, src_t, cross_t, load_sem, pair_send, pair_recv, send_sem, recv_sem, edge_send, edge_recv):
    nblk, nchan, _, nwin, _ = spec.shape
    nsrc, depth = plane.shape[0], 2 * nwin
    n, _, many, _, _ = give.shape
    per = n // nblk
    size = outer * inner * 2
    me = lax.axis_index("chan")
    core, chip = me % 2, me // 2
    j, i = chip % inner, chip // inner
    line_j, line_i = (j, inner, 2), (i, outer, 2 * inner)
    teeth, spine = (line_j, line_i), (line_i, line_j)
    partner = me + 1 - 2 * core
    pitch, cpitch = FB + 1, 2 * nsrc + 1

    def root(q, odd):
        length = teeth[q][1]
        return 0 if length == 1 else (length - 1) // 2 + odd

    reach = [max(root(q, 1), teeth[q][1] - 1 - root(q, 0)) for q in range(2)]
    rooted = reach
    summed = [rooted[q] + spine[q][1] - 1 for q in range(2)]

    def lag(hops):
        return (HALF_LAG * hops + 1) // 2

    spread_at = max(lag(summed[q] + reach[q]) for q in range(2))
    settled = spread_at + SETTLE
    loaded = max(per - AHEAD, 0)
    turn_at = min(loaded + 1, settled)
    at_root = [[teeth[q][0] == root(q, odd) for odd in range(2)] for q in range(2)]

    def load(b):
        return pltpu.make_async_copy(spec_ref.at[:, :, :, pl.ds(b * FB, FB)], spec.at[b], load_sem.at[1 + b])

    small = [pltpu.make_async_copy(src_hbm, src_ref, load_sem.at[1 + nblk]),
             pltpu.make_async_copy(valid_hbm, valid_ref, load_sem.at[2 + nblk])]
    for copy in small:
        copy.start()
    load_first = pltpu.make_async_copy(spec_ref.at[:, :, :, pl.ds(0, FB)], first, load_sem.at[0])
    load_first.start()
    for b in range(nblk):
        load(b).start()

    barrier = pltpu.get_barrier_semaphore()

    def greet(there):
        pl.semaphore_signal(barrier, inc=1, device_id={"chan": there}, device_id_type=MESH)

    greet(partner)
    count = jnp.int32(1)
    for pos, length, stride in (line_j, line_i, (me, size, 1)):
        @pl.when(pos > 0)
        def _():
            greet(me - stride)

        @pl.when(pos < length - 1)
        def _():
            greet(me + stride)

        count = count + (pos > 0).astype(jnp.int32) + (pos < length - 1).astype(jnp.int32)

    for copy in small:
        copy.wait()
    raw = valid_ref[...].astype(jnp.float32)
    flags[...] = jnp.concatenate([raw, raw], axis=1)
    by_window = jnp.transpose(flags[...])[0:nwin].astype(jnp.bfloat16)
    place = lax.broadcasted_iota(jnp.int32, (nchan, FB), 0)
    for s in range(nsrc):
        hot = (place == src_ref[s] - me * nchan).astype(jnp.bfloat16)
        plane[s] = jnp.dot(by_window, hot, preferred_element_type=jnp.float32).astype(jnp.bfloat16)

    pl.semaphore_wait(barrier, count)

    def edge_flags(up):
        side, eight = (0, nchan - 8) if up else (1, 0)
        return pltpu.make_async_remote_copy(
            src_ref=valid_ref.at[pl.ds(eight, 8)], dst_ref=halo_valid.at[side],
            send_sem=edge_send.at[side, nblk], recv_sem=edge_recv.at[side, nblk],
            device_id={"chan": me + 1 if up else me - 1}, device_id_type=MESH)

    def edge(up, b):
        side, rows = (0, nchan - HALO) if up else (1, 0)
        return pltpu.make_async_remote_copy(
            src_ref=spec_ref.at[pl.ds(rows, HALO), :, :, pl.ds(b * FB, FB)], dst_ref=halo.at[side, b],
            send_sem=edge_send.at[side, b], recv_sem=edge_recv.at[side, b],
            device_id={"chan": me + 1 if up else me - 1}, device_id_type=MESH)

    def to_neighbours(act, blocks=()):
        @pl.when(me < size - 1)
        def _():
            for copy in [edge(True, b) for b in blocks] or [edge_flags(True)]:
                act(copy)

        @pl.when(me > 0)
        def _():
            for copy in [edge(False, b) for b in blocks] or [edge_flags(False)]:
                act(copy)

    def from_neighbours(blocks=()):
        @pl.when(me > 0)
        def _():
            for copy in [edge(True, b) for b in blocks] or [edge_flags(True)]:
                copy.wait_recv()

        @pl.when(me < size - 1)
        def _():
            for copy in [edge(False, b) for b in blocks] or [edge_flags(False)]:
                copy.wait_recv()

    to_neighbours(lambda copy: copy.start())
    if FIRST_EDGES:
        to_neighbours(lambda copy: copy.start(), range(FIRST_EDGES))

    def across(k):
        return pltpu.make_async_remote_copy(
            src_ref=give.at[k], dst_ref=part.at[k], send_sem=pair_send.at[0], recv_sem=pair_recv.at[0, k],
            device_id={"chan": partner}, device_id_type=MESH)

    def back(k, half):
        return pltpu.make_async_remote_copy(
            src_ref=gathered.at[k, half], dst_ref=gathered.at[k, half], send_sem=pair_send.at[1],
            recv_sem=pair_recv.at[1, k], device_id={"chan": partner}, device_id_type=MESH)

    def remote(src, dst, kind, q, odd, k, there):
        return pltpu.make_async_remote_copy(
            src_ref=src, dst_ref=dst, send_sem=send_sem.at[kind, q, odd], recv_sem=recv_sem.at[kind, q, k],
            device_id={"chan": there}, device_id_type=MESH)

    def toward(q, up, odd, k):
        there = me + teeth[q][2] if up else me - teeth[q][2]
        return remote(own.at[k, q], inward.at[0 if up else 1, k, q], IN_UP if up else IN_DOWN, q, odd, k, there)

    def onward(q, up, odd, k, src):
        there = me + spine[q][2] if up else me - spine[q][2]
        return remote(src, along.at[0 if up else 1, k, q], ON_UP if up else ON_DOWN, q, odd, k, there)

    def outward(q, up, odd, k):
        there = me + teeth[q][2] if up else me - teeth[q][2]
        block = gathered.at[k, core, q]
        return remote(block, block, OUT_UP if up else OUT_DOWN, q, odd, k, there)

    def prepare(block, k):
        for q in range(2):
            for m in range(many):
                s = ((k % per) * 2 + q) * many + m
                held = jnp.clip(src_ref[s] - me * nchan, 0, nchan - 1)
                mask = plane[s]
                give[k, q, m] = block[held, 1 - core] * mask
                own[k, q, m] = block[held, core] * mask
        across(k).start()

    def guarded(k, also, run):
        @pl.when((k >= 0) & (k < n) & also)
        def _():
            run()

    def enter(k, odd):
        across(k).wait_recv()
        own[k] = own[k] + part[k]
        for q in range(2):
            pos, length, _ = teeth[q]
            if root(q, odd) > 0:
                @pl.when(pos == 0)
                def _():
                    toward(q, True, odd, k).start()

            if root(q, odd) < length - 1:
                @pl.when(pos == length - 1)
                def _():
                    toward(q, False, odd, k).start()

    def relay_in(q, t, p):
        pos, length, _ = teeth[q]
        for up in (True, False):
            for here in range(1, length - 1):
                steps = here if up else length - 1 - here
                odd = (p - lag(steps)) % 2
                k = t - lag(steps)
                if (here < root(q, odd)) if up else (here > root(q, odd)):
                    def run():
                        toward(q, up, odd, k).wait_recv()
                        own[k, q] = own[k, q] + inward[0 if up else 1, k, q]
                        toward(q, up, odd, k).start()

                    guarded(k, pos == here, run)

    def reach_root(q, k, odd):
        length = teeth[q][1]
        at, span, _ = spine[q]
        ways = []
        if root(q, odd) > 0:
            ways.append(0)
        if root(q, odd) < length - 1:
            ways.append(1)
        for way in ways:
            toward(q, way == 0, odd, k).wait_recv()
        if ways:
            total = own[k, q]
            for way in ways:
                total = total + inward[way, k, q]
            own[k, q] = total
        if span > 1:
            @pl.when(at == 0)
            def _():
                onward(q, True, odd, k, own.at[k, q]).start()

            @pl.when(at == span - 1)
            def _():
                onward(q, False, odd, k, own.at[k, q]).start()

    def relay_on(q, t, p):
        at, span, _ = spine[q]
        for up in (True, False):
            for here in range(1, span - 1):
                steps = here if up else span - 1 - here
                odd = (p - lag(rooted[q] + steps)) % 2
                k = t - lag(rooted[q] + steps)

                def run():
                    way = 0 if up else 1
                    onward(q, up, odd, k, own.at[k, q]).wait_recv()
                    passed[way, k, q] = own[k, q] + along[way, k, q]
                    onward(q, up, odd, k, passed.at[way, k, q]).start()

                guarded(k, at_root[q][odd] & (at == here), run)

    def finish(q, k, odd):
        pos, length, _ = teeth[q]
        at, span, _ = spine[q]
        if span == 1:
            gathered[k, core, q] = own[k, q]
        else:
            @pl.when(at == 0)
            def _():
                onward(q, False, odd, k, own.at[k, q]).wait_recv()
                gathered[k, core, q] = own[k, q] + along[1, k, q]

            @pl.when(at == span - 1)
            def _():
                onward(q, True, odd, k, own.at[k, q]).wait_recv()
                gathered[k, core, q] = own[k, q] + along[0, k, q]

            if span > 2:
                @pl.when((at > 0) & (at < span - 1))
                def _():
                    gathered[k, core, q] = own[k, q] + along[0, k, q] + along[1, k, q]
        if root(q, odd) < length - 1:
            outward(q, True, odd, k).start()
        if root(q, odd) > 0:
            outward(q, False, odd, k).start()

    def spread(q, t, p):
        pos, length, _ = teeth[q]
        for far in range(reach[q], 0, -1):
            odd = (p - lag(summed[q] + far)) % 2
            k = t - lag(summed[q] + far)
            for up in (True, False):
                here = root(q, odd) + far if up else root(q, odd) - far
                if 0 <= here < length:
                    def run():
                        outward(q, up, odd, k).wait_recv()
                        if (here < length - 1) if up else (here > 0):
                            outward(q, up, odd, k).start()

                    guarded(k, pos == here, run)

    def all_sent():
        def drain(block, sem):
            pltpu.make_async_remote_copy(
                src_ref=block, dst_ref=block, send_sem=sem, recv_sem=pair_recv.at[0, 0],
                device_id={"chan": partner}, device_id_type=MESH).wait_send()

        drain(give, pair_send.at[0])
        drain(give, pair_send.at[1])
        for q in range(2):
            pos, length, _ = teeth[q]
            at, span, _ = spine[q]
            for odd in range(2):
                r = root(q, odd)
                for kind, when in ((IN_UP, pos < r), (IN_DOWN, pos > r),
                                   (ON_UP, (pos == r) & (at < span - 1)), (ON_DOWN, (pos == r) & (at > 0)),
                                   (OUT_UP, (pos >= r) & (pos < length - 1)), (OUT_DOWN, (pos <= r) & (pos > 0))):
                    @pl.when(when)
                    def _():
                        drain(own.at[pl.ds(0, n // 2), q], send_sem.at[kind, q, odd])

    sign = jnp.where(lax.broadcasted_iota(jnp.int32, (1, depth), 1) < nwin, -1.0, 1.0)

    def settle(k):
        base = ((k // per) % 2) * (2 * nsrc * pitch)
        for q in range(2):
            for m in range(many):
                both = jnp.concatenate([gathered[k, 0, q, m], gathered[k, 1, q, m]], axis=0)
                x = jnp.transpose(both).astype(jnp.float32)
                s = ((k % per) * 2 + q) * many + m
                src_t[pl.ds(base + s * pitch, FB)] = x
                src_t[pl.ds(base + (s + nsrc) * pitch, FB)] = pltpu.roll(x, nwin, axis=1) * sign

    def turn(k):
        b, lot = k // per, k % per
        base = b * (nrow * pitch)
        count = nchan // per
        for u in range(count):
            c = lot * count + u
            x = jnp.transpose(spec[b, c].reshape(depth, FB)).astype(jnp.float32) * flags[pl.ds(c, 1)]
            chan_t[pl.ds(base + (c + HALO) * pitch, FB)] = x

    def turn_edges(b):
        from_neighbours([b])
        base = b * (nrow * pitch)
        for h in range(2 * HALO):
            side, c = h // HALO, h % HALO
            row = halo_valid[side][(8 - HALO + c) if side == 0 else c][None].astype(jnp.float32)
            row = jnp.concatenate([row, row], axis=1)
            x = jnp.transpose(halo[side, b, c].reshape(depth, FB)).astype(jnp.float32) * row
            chan_t[pl.ds(base + (c + side * (HALO + nchan)) * pitch, FB)] = x

    nothing = jnp.zeros((2 * nsrc, depth), jnp.bfloat16)

    def correlate(b, f):
        def rows(ref, base, count, at):
            return ref[pl.ds(base + at, count, stride=pitch)].astype(jnp.bfloat16)

        right = [rows(chan_t, b * (nrow * pitch), nrow, f + u) for u in range(2)]
        left = [rows(src_t, (b % 2) * (2 * nsrc * pitch), 2 * nsrc, f + u) for u in range(2)]
        left = jnp.concatenate([jnp.concatenate([left[0], nothing], axis=1),
                                jnp.concatenate([nothing, left[1]], axis=1)], axis=0)
        both = lax.dot_general(left, jnp.concatenate(right, axis=1), (((1,), (1,)), ((), ())),
                               preferred_element_type=jnp.float32)
        for u in range(2):
            at = (b % 2) * (FB * cpitch) + (f + u) * cpitch
            cross_t[pl.ds(at, 2 * nsrc), 0:nrow] = both[2 * nsrc * u:2 * nsrc * (u + 1)]

    ahead = (lax.broadcasted_iota(jnp.int32, (nchan, FB), 1)
             - lax.broadcasted_iota(jnp.int32, (nchan, FB), 0))
    band = ((ahead >= 0) & (ahead <= 2 * HALO)).astype(jnp.bfloat16)
    apart = jnp.zeros_like(band)
    bands = jnp.concatenate([jnp.concatenate([band, apart], axis=1),
                             jnp.concatenate([apart, band], axis=1)], axis=0)

    def smooth(b, s):
        base = (b % 2) * (FB * cpitch)
        flats = []
        for u in range(2):
            parts = [cross_t[pl.ds(base + odd * cpitch + s + u + half * nsrc, FB // 2, stride=2 * cpitch)]
                     for odd in range(2) for half in range(2)]
            flats.append(jnp.concatenate(parts, axis=0).astype(jnp.bfloat16))
        total = lax.dot_general(bands, jnp.concatenate(flats, axis=1), (((1,), (1,)), ((), ())),
                                preferred_element_type=jnp.float32).astype(jnp.bfloat16)
        rows = pl.ds(pl.multiple_of(s * nchan, nchan), 2 * nchan)
        flat_ref[rows, pl.ds(pl.multiple_of(b * FB, FB), FB)] = total[:, 0:FB]
        flat_ref[rows, pl.ds(pl.multiple_of((nblk + b) * FB, FB), FB)] = total[:, FB:]

    load_first.wait()

    def prepare_first(k, carry):
        prepare(first, k)
        return carry

    lax.fori_loop(0, per, prepare_first, 0, unroll=True)

    @pl.when(me == 0)
    def _():
        halo[0] = jnp.zeros(halo.shape[1:], halo.dtype)
        halo_valid[0] = jnp.zeros(halo_valid.shape[1:], halo_valid.dtype)

    @pl.when(me == size - 1)
    def _():
        halo[1] = jnp.zeros(halo.shape[1:], halo.dtype)
        halo_valid[1] = jnp.zeros(halo_valid.shape[1:], halo_valid.dtype)

    def clear():
        def some(f, carry):
            cross_t[pl.ds(pl.multiple_of(f * 8 * cpitch, 8), 8 * cpitch)] = jnp.zeros((8 * cpitch, FB), jnp.float32)
            return carry

        lax.fori_loop(0, 2 * FB // 8, some, 0)
        for slot in range(nblk):
            for c in range(nchan + 2 * HALO, nrow):
                chan_t[pl.ds((slot * nrow + c) * pitch, pitch)] = jnp.zeros((pitch, depth), jnp.float32)

    def step(t, p):
        @pl.when(t == loaded)
        def _():
            for b in range(nblk):
                load(b).wait()

        @pl.when(t == loaded + 1)
        def _():
            clear()
            from_neighbours()

        for b in range(FIRST_EDGES, nblk):
            @pl.when(t == settled + per * (b + 1) - EARLY)
            def _():
                to_neighbours(lambda copy: copy.start(), [b])

        guarded(t, True, functools.partial(enter, t, p))
        for q in range(2):
            relay_in(q, t, p)
        for q in range(2):
            at = lag(rooted[q])
            odd = (p - at) % 2
            guarded(t - at, at_root[q][odd], functools.partial(reach_root, q, t - at, odd))
        now = t - settled

        @pl.when((now >= 0) & (now < per))
        def _():
            back(now, 1 - core).wait_recv()
            settle(now)

        @pl.when((now >= per) & (now < n))
        def _():
            back(now, 1 - core).wait_recv()
            b, lot = now // per - 1, now % per
            for u in range(0, nsrc // per, 2):
                smooth(jnp.maximum(b - 1, 0), lot * (nsrc // per) + u)
            for u in range(0, FB // per, 2):
                correlate(b, lot * (FB // per) + u)
            settle(now)

        for q in range(2):
            relay_on(q, t, p)
        for q in range(2):
            at = lag(summed[q])
            odd = (p - at) % 2
            guarded(t - at, at_root[q][odd], functools.partial(finish, q, t - at, odd))
        for q in range(2):
            spread(q, t, p)
        guarded(t - spread_at, True, lambda: back(t - spread_at, core).start())
        later = t + AHEAD
        guarded(later, later >= per, lambda: prepare(spec.at[later // per], later))
        guarded(t - turn_at, True, functools.partial(turn, t - turn_at))
        for b in range(nblk):
            @pl.when(t == settled + per * (b + 1) - 1)
            def _():
                turn_edges(b)


    def steps(tt, carry):
        for p in range(2):
            step(2 * tt + p, p)
        return carry

    total = n + settled
    lax.fori_loop(0, total // 2, steps, 0)
    if total % 2:
        step(jnp.int32(total - 1), (total - 1) % 2)

    for s in range(0, nsrc if nblk > 1 else 0, 2):
        smooth(nblk - 2, s)
    for f in range(0, FB, 2):
        correlate(nblk - 1, f)
    for s in range(0, nsrc, 2):
        smooth(nblk - 1, s)
    all_sent()
    to_neighbours(lambda copy: copy.wait_send())
    to_neighbours(lambda copy: copy.wait_send(), range(nblk))


def lag_kernel(scale, flat_ref, table_ref, out_ref, lags, sems):
    half = table_ref.shape[1]
    rows = lags.shape[1]
    copies = []
    for piece in range(PIECES):
        at = pl.ds(piece * rows, rows)
        even = jnp.dot(flat_ref[at, 0:half], table_ref[0:half], preferred_element_type=jnp.float32)
        odd = jnp.dot(flat_ref[at, half:], table_ref[half:], preferred_element_type=jnp.float32)
        lags[piece, :, 0:half] = (even + odd) * scale
        lags[piece, :, half:] = (even - odd) * scale
        copy = pltpu.make_async_copy(lags.at[piece], out_ref.at[at], sems.at[piece])
        copy.start()
        copies.append(copy)
    for copy in copies:
        copy.wait()


def local(size, spectra, valid, sources):
    nchan, _, nwin, nbins = spectra.shape
    nsrc = sources.shape[0]
    depth, nlags = 2 * nwin, 2 * nbins
    vmem = pl.BlockSpec(memory_space=pltpu.VMEM)

    chips = size // 2
    inner = 1
    while (2 * inner) ** 2 <= chips and chips % (2 * inner) == 0:
        inner *= 2
    outer = chips // inner
    nblk = nbins // FB
    many = MANY
    n = nblk * nsrc // (2 * many)
    nrow = -(-(nchan + 2 * HALO) // 16) * 16
    pitch, cpitch = FB + 1, 2 * nsrc + 1
    chunks = lambda *lead: pltpu.VMEM(lead + (n, 2, many, nwin, FB), jnp.bfloat16)
    flat = pl.pallas_call(
        functools.partial(cross_kernel, outer, inner, nrow),
        out_shape=pltpu.VMEM((nsrc * nchan, nlags), jnp.bfloat16),
        in_specs=[pl.BlockSpec(memory_space=pltpu.MemorySpace.HBM)] * 3,
        out_specs=vmem,
        scratch_shapes=[pltpu.SMEM((nsrc,), jnp.int32), pltpu.VMEM((nchan, nwin), jnp.int32),
                        pltpu.VMEM((nchan, 2, nwin, FB), jnp.bfloat16),
                        pltpu.VMEM((nblk, nchan, 2, nwin, FB), jnp.bfloat16),
                        pltpu.VMEM((2, nblk, HALO, 2, nwin, FB), jnp.bfloat16),
                        pltpu.VMEM((2, 8, nwin), jnp.int32),
                        pltpu.VMEM((nchan, depth), jnp.float32),
                        pltpu.VMEM((nsrc, nwin, FB), jnp.bfloat16),
                        chunks(), chunks(), chunks(), chunks(2), chunks(2), chunks(2),
                        pltpu.VMEM((n, 2, 2, many, nwin, FB), jnp.bfloat16),
                        pltpu.VMEM((nblk * nrow * pitch, depth), jnp.float32),
                        pltpu.VMEM((2 * 2 * nsrc * pitch, depth), jnp.float32),
                        pltpu.VMEM((2 * FB * cpitch, FB), jnp.float32),
                        pltpu.SemaphoreType.DMA((3 + nblk,)),
                        pltpu.SemaphoreType.DMA((2,)), pltpu.SemaphoreType.DMA((2, n)),
                        pltpu.SemaphoreType.DMA((6, 2, 2)), pltpu.SemaphoreType.DMA((6, 2, n)),
                        pltpu.SemaphoreType.DMA((2, nblk + 1)), pltpu.SemaphoreType.DMA((2, nblk + 1))],
        compiler_params=pltpu.CompilerParams(
            collective_id=0, has_side_effects=True, vmem_limit_bytes=56 << 20),
        name="cross",
    )(sources, valid, spectra)

    rows = nsrc * nchan // PIECES
    lags = pl.pallas_call(
        functools.partial(lag_kernel, 1.0 / (nwin * (2 * HALO + 1.0))),
        out_shape=jax.ShapeDtypeStruct((nsrc * nchan, nlags), jnp.float32),
        in_specs=[vmem, vmem],
        out_specs=pl.BlockSpec(memory_space=pltpu.MemorySpace.HBM),
        scratch_shapes=[pltpu.VMEM((PIECES, rows, nlags), jnp.float32), pltpu.SemaphoreType.DMA((PIECES,))],
        compiler_params=pltpu.CompilerParams(vmem_limit_bytes=24 << 20),
        name="lags",
    )(flat, jnp.asarray(make_table(nbins, nlags)))
    return lags.reshape(nsrc, nchan, nlags)


def solution(mesh):
    in_specs = (P(("grp", "chan"), None, None, None), P(("grp", "chan"), None), P("grp"))
    out_specs = P("grp", "chan", None)
    return jax.shard_map(functools.partial(local, mesh.shape["chan"]), mesh=mesh,
                         in_specs=in_specs, out_specs=out_specs, check_vma=False)
```

```python
import functools

import jax
import jax.numpy as jnp
import numpy as np
from jax import lax
from jax.experimental import pallas as pl
from jax.experimental.pallas import tpu as pltpu
from jax.sharding import PartitionSpec as P

MESH = pl.DeviceIdType.MESH
HALO = 2
HALF_LAG = 6
FIRST_EDGES = 1
AHEAD = 2
PIECES = 8
SETTLE = 2
EARLY = 5
FB = 128
MANY = 2
IN_UP, IN_DOWN, ON_UP, ON_DOWN, OUT_UP, OUT_DOWN = range(6)


def make_table(nbins, nlags):
    freq = np.arange(nbins, dtype=np.int64)
    phase = (freq[:, None] * np.arange(nlags, dtype=np.int64)[None, :]) % nlags
    angle = 2.0 * np.pi * phase / nlags
    weight = np.where(freq == 0, 1.0, 2.0) / nlags
    table = np.concatenate([weight[:, None] * np.cos(angle), -weight[:, None] * np.sin(angle)])
    order = np.concatenate([blk * FB + half * nbins + np.arange(odd, FB, 2)
                            for odd in range(2) for blk in range(nbins // FB) for half in range(2)])
    return table[order, :nlags // 2].astype(np.float32).astype(jnp.bfloat16)


def cross_kernel(outer, inner, nrow, src_hbm, valid_hbm, spec_ref, flat_ref, src_ref, valid_ref,
                 first, spec, halo, halo_valid, flags, plane, give, own, part, inward, along, passed, gathered,
                 chan_t, src_t, cross_t, load_sem, pair_send, pair_recv, send_sem, recv_sem, edge_send, edge_recv):
    nblk, nchan, _, nwin, _ = spec.shape
    nsrc, depth = plane.shape[0], 2 * nwin
    n, _, many, _, _ = give.shape
    per = n // nblk
    size = outer * inner * 2
    me = lax.axis_index("chan")
    core, chip = me % 2, me // 2
    j, i = chip % inner, chip // inner
    line_j, line_i = (j, inner, 2), (i, outer, 2 * inner)
    teeth, spine = (line_j, line_i), (line_i, line_j)
    partner = me + 1 - 2 * core
    pitch, cpitch = FB + 1, 2 * nsrc + 1

    def root(q, odd):
        length = teeth[q][1]
        return 0 if length == 1 else (length - 1) // 2 + odd

    reach = [max(root(q, 1), teeth[q][1] - 1 - root(q, 0)) for q in range(2)]
    rooted = reach
    summed = [rooted[q] + spine[q][1] - 1 for q in range(2)]

    def lag(hops):
        return (HALF_LAG * hops + 1) // 2

    spread_at = max(lag(summed[q] + reach[q]) for q in range(2))
    settled = spread_at + SETTLE
    loaded = max(per - AHEAD, 0)
    turn_at = min(loaded + 1, settled)
    at_root = [[teeth[q][0] == root(q, odd) for odd in range(2)] for q in range(2)]

    def load(b):
        return pltpu.make_async_copy(spec_ref.at[:, :, :, pl.ds(b * FB, FB)], spec.at[b], load_sem.at[1 + b])

    small = [pltpu.make_async_copy(src_hbm, src_ref, load_sem.at[1 + nblk]),
             pltpu.make_async_copy(valid_hbm, valid_ref, load_sem.at[2 + nblk])]
    for copy in small:
        copy.start()
    load_first = pltpu.make_async_copy(spec_ref.at[:, :, :, pl.ds(0, FB)], first, load_sem.at[0])
    load_first.start()
    for b in range(nblk):
        load(b).start()

    barrier = pltpu.get_barrier_semaphore()

    def greet(there):
        pl.semaphore_signal(barrier, inc=1, device_id={"chan": there}, device_id_type=MESH)

    greet(partner)
    count = jnp.int32(1)
    for pos, length, stride in (line_j, line_i, (me, size, 1)):
        @pl.when(pos > 0)
        def _():
            greet(me - stride)

        @pl.when(pos < length - 1)
        def _():
            greet(me + stride)

        count = count + (pos > 0).astype(jnp.int32) + (pos < length - 1).astype(jnp.int32)

    for copy in small:
        copy.wait()
    raw = valid_ref[...].astype(jnp.float32)
    flags[...] = jnp.concatenate([raw, raw], axis=1)
    by_window = jnp.transpose(flags[...])[0:nwin].astype(jnp.bfloat16)
    place = lax.broadcasted_iota(jnp.int32, (nchan, FB), 0)
    for s in range(nsrc):
        hot = (place == src_ref[s] - me * nchan).astype(jnp.bfloat16)
        plane[s] = jnp.dot(by_window, hot, preferred_element_type=jnp.float32).astype(jnp.bfloat16)

    pl.semaphore_wait(barrier, count)

    def edge_flags(up):
        side, eight = (0, nchan - 8) if up else (1, 0)
        return pltpu.make_async_remote_copy(
            src_ref=valid_ref.at[pl.ds(eight, 8)], dst_ref=halo_valid.at[side],
            send_sem=edge_send.at[side, nblk], recv_sem=edge_recv.at[side, nblk],
            device_id={"chan": me + 1 if up else me - 1}, device_id_type=MESH)

    def edge(up, b):
        side, rows = (0, nchan - HALO) if up else (1, 0)
        return pltpu.make_async_remote_copy(
            src_ref=spec_ref.at[pl.ds(rows, HALO), :, :, pl.ds(b * FB, FB)], dst_ref=halo.at[side, b],
            send_sem=edge_send.at[side, b], recv_sem=edge_recv.at[side, b],
            device_id={"chan": me + 1 if up else me - 1}, device_id_type=MESH)

    def to_neighbours(act, blocks=()):
        @pl.when(me < size - 1)
        def _():
            for copy in [edge(True, b) for b in blocks] or [edge_flags(True)]:
                act(copy)

        @pl.when(me > 0)
        def _():
            for copy in [edge(False, b) for b in blocks] or [edge_flags(False)]:
                act(copy)

    def from_neighbours(blocks=()):
        @pl.when(me > 0)
        def _():
            for copy in [edge(True, b) for b in blocks] or [edge_flags(True)]:
                copy.wait_recv()

        @pl.when(me < size - 1)
        def _():
            for copy in [edge(False, b) for b in blocks] or [edge_flags(False)]:
                copy.wait_recv()

    to_neighbours(lambda copy: copy.start())
    if FIRST_EDGES:
        to_neighbours(lambda copy: copy.start(), range(FIRST_EDGES))

    def across(k):
        return pltpu.make_async_remote_copy(
            src_ref=give.at[k], dst_ref=part.at[k], send_sem=pair_send.at[0], recv_sem=pair_recv.at[0, k],
            device_id={"chan": partner}, device_id_type=MESH)

    def back(k, half):
        return pltpu.make_async_remote_copy(
            src_ref=gathered.at[k, half], dst_ref=gathered.at[k, half], send_sem=pair_send.at[1],
            recv_sem=pair_recv.at[1, k], device_id={"chan": partner}, device_id_type=MESH)

    def remote(src, dst, kind, q, odd, k, there):
        return pltpu.make_async_remote_copy(
            src_ref=src, dst_ref=dst, send_sem=send_sem.at[kind, q, odd], recv_sem=recv_sem.at[kind, q, k],
            device_id={"chan": there}, device_id_type=MESH)

    def toward(q, up, odd, k):
        there = me + teeth[q][2] if up else me - teeth[q][2]
        return remote(own.at[k, q], inward.at[0 if up else 1, k, q], IN_UP if up else IN_DOWN, q, odd, k, there)

    def onward(q, up, odd, k, src):
        there = me + spine[q][2] if up else me - spine[q][2]
        return remote(src, along.at[0 if up else 1, k, q], ON_UP if up else ON_DOWN, q, odd, k, there)

    def outward(q, up, odd, k):
        there = me + teeth[q][2] if up else me - teeth[q][2]
        block = gathered.at[k, core, q]
        return remote(block, block, OUT_UP if up else OUT_DOWN, q, odd, k, there)

    def prepare(block, k):
        for q in range(2):
            for m in range(many):
                s = ((k % per) * 2 + q) * many + m
                held = jnp.clip(src_ref[s] - me * nchan, 0, nchan - 1)
                mask = plane[s]
                give[k, q, m] = block[held, 1 - core] * mask
                own[k, q, m] = block[held, core] * mask
        across(k).start()

    def guarded(k, also, run):
        @pl.when((k >= 0) & (k < n) & also)
        def _():
            run()

    def enter(k, odd):
        across(k).wait_recv()
        own[k] = own[k] + part[k]
        for q in range(2):
            pos, length, _ = teeth[q]
            if root(q, odd) > 0:
                @pl.when(pos == 0)
                def _():
                    toward(q, True, odd, k).start()

            if root(q, odd) < length - 1:
                @pl.when(pos == length - 1)
                def _():
                    toward(q, False, odd, k).start()

    def relay_in(q, t, p):
        pos, length, _ = teeth[q]
        for up in (True, False):
            for here in range(1, length - 1):
                steps = here if up else length - 1 - here
                odd = (p - lag(steps)) % 2
                k = t - lag(steps)
                if (here < root(q, odd)) if up else (here > root(q, odd)):
                    def run():
                        toward(q, up, odd, k).wait_recv()
                        own[k, q] = own[k, q] + inward[0 if up else 1, k, q]
                        toward(q, up, odd, k).start()

                    guarded(k, pos == here, run)

    def reach_root(q, k, odd):
        length = teeth[q][1]
        at, span, _ = spine[q]
        ways = []
        if root(q, odd) > 0:
            ways.append(0)
        if root(q, odd) < length - 1:
            ways.append(1)
        for way in ways:
            toward(q, way == 0, odd, k).wait_recv()
        if ways:
            total = own[k, q]
            for way in ways:
                total = total + inward[way, k, q]
            own[k, q] = total
        if span > 1:
            @pl.when(at == 0)
            def _():
                onward(q, True, odd, k, own.at[k, q]).start()

            @pl.when(at == span - 1)
            def _():
                onward(q, False, odd, k, own.at[k, q]).start()

    def relay_on(q, t, p):
        at, span, _ = spine[q]
        for up in (True, False):
            for here in range(1, span - 1):
                steps = here if up else span - 1 - here
                odd = (p - lag(rooted[q] + steps)) % 2
                k = t - lag(rooted[q] + steps)

                def run():
                    way = 0 if up else 1
                    onward(q, up, odd, k, own.at[k, q]).wait_recv()
                    passed[way, k, q] = own[k, q] + along[way, k, q]
                    onward(q, up, odd, k, passed.at[way, k, q]).start()

                guarded(k, at_root[q][odd] & (at == here), run)

    def finish(q, k, odd):
        pos, length, _ = teeth[q]
        at, span, _ = spine[q]
        if span == 1:
            gathered[k, core, q] = own[k, q]
        else:
            @pl.when(at == 0)
            def _():
                onward(q, False, odd, k, own.at[k, q]).wait_recv()
                gathered[k, core, q] = own[k, q] + along[1, k, q]

            @pl.when(at == span - 1)
            def _():
                onward(q, True, odd, k, own.at[k, q]).wait_recv()
                gathered[k, core, q] = own[k, q] + along[0, k, q]

            if span > 2:
                @pl.when((at > 0) & (at < span - 1))
                def _():
                    gathered[k, core, q] = own[k, q] + along[0, k, q] + along[1, k, q]
        if root(q, odd) < length - 1:
            outward(q, True, odd, k).start()
        if root(q, odd) > 0:
            outward(q, False, odd, k).start()

    def spread(q, t, p):
        pos, length, _ = teeth[q]
        for far in range(reach[q], 0, -1):
            odd = (p - lag(summed[q] + far)) % 2
            k = t - lag(summed[q] + far)
            for up in (True, False):
                here = root(q, odd) + far if up else root(q, odd) - far
                if 0 <= here < length:
                    def run():
                        outward(q, up, odd, k).wait_recv()
                        if (here < length - 1) if up else (here > 0):
                            outward(q, up, odd, k).start()

                    guarded(k, pos == here, run)

    def all_sent():
        def drain(block, sem):
            pltpu.make_async_remote_copy(
                src_ref=block, dst_ref=block, send_sem=sem, recv_sem=pair_recv.at[0, 0],
                device_id={"chan": partner}, device_id_type=MESH).wait_send()

        drain(give, pair_send.at[0])
        drain(give, pair_send.at[1])
        for q in range(2):
            pos, length, _ = teeth[q]
            at, span, _ = spine[q]
            for odd in range(2):
                r = root(q, odd)
                for kind, when in ((IN_UP, pos < r), (IN_DOWN, pos > r),
                                   (ON_UP, (pos == r) & (at < span - 1)), (ON_DOWN, (pos == r) & (at > 0)),
                                   (OUT_UP, (pos >= r) & (pos < length - 1)), (OUT_DOWN, (pos <= r) & (pos > 0))):
                    @pl.when(when)
                    def _():
                        drain(own.at[pl.ds(0, n // 2), q], send_sem.at[kind, q, odd])

    sign = jnp.where(lax.broadcasted_iota(jnp.int32, (1, depth), 1) < nwin, -1.0, 1.0)

    def settle(k):
        base = ((k // per) % 2) * (2 * nsrc * pitch)
        for q in range(2):
            for m in range(many):
                both = jnp.concatenate([gathered[k, 0, q, m], gathered[k, 1, q, m]], axis=0)
                x = jnp.transpose(both).astype(jnp.float32)
                s = ((k % per) * 2 + q) * many + m
                src_t[pl.ds(base + s * pitch, FB)] = x
                src_t[pl.ds(base + (s + nsrc) * pitch, FB)] = pltpu.roll(x, nwin, axis=1) * sign

    def turn(k):
        b, lot = k // per, k % per
        base = b * (nrow * pitch)
        count = nchan // per
        for u in range(count):
            c = lot * count + u
            x = jnp.transpose(spec[b, c].reshape(depth, FB)).astype(jnp.float32) * flags[pl.ds(c, 1)]
            chan_t[pl.ds(base + (c + HALO) * pitch, FB)] = x

    def turn_edges(b):
        from_neighbours([b])
        base = b * (nrow * pitch)
        for h in range(2 * HALO):
            side, c = h // HALO, h % HALO
            row = halo_valid[side][(8 - HALO + c) if side == 0 else c][None].astype(jnp.float32)
            row = jnp.concatenate([row, row], axis=1)
            x = jnp.transpose(halo[side, b, c].reshape(depth, FB)).astype(jnp.float32) * row
            chan_t[pl.ds(base + (c + side * (HALO + nchan)) * pitch, FB)] = x

    nothing = jnp.zeros((2 * nsrc, depth), jnp.bfloat16)

    def correlate(b, f):
        def rows(ref, base, count, at):
            return ref[pl.ds(base + at, count, stride=pitch)].astype(jnp.bfloat16)

        right = [rows(chan_t, b * (nrow * pitch), nrow, f + u) for u in range(2)]
        left = [rows(src_t, (b % 2) * (2 * nsrc * pitch), 2 * nsrc, f + u) for u in range(2)]
        left = jnp.concatenate([jnp.concatenate([left[0], nothing], axis=1),
                                jnp.concatenate([nothing, left[1]], axis=1)], axis=0)
        both = lax.dot_general(left, jnp.concatenate(right, axis=1), (((1,), (1,)), ((), ())),
                               preferred_element_type=jnp.float32)
        for u in range(2):
            at = (b % 2) * (FB * cpitch) + (f + u) * cpitch
            cross_t[pl.ds(at, 2 * nsrc), 0:nrow] = both[2 * nsrc * u:2 * nsrc * (u + 1)]

    ahead = (lax.broadcasted_iota(jnp.int32, (nchan, FB), 1)
             - lax.broadcasted_iota(jnp.int32, (nchan, FB), 0))
    band = ((ahead >= 0) & (ahead <= 2 * HALO)).astype(jnp.bfloat16)
    apart = jnp.zeros_like(band)
    bands = jnp.concatenate([jnp.concatenate([band, apart], axis=1),
                             jnp.concatenate([apart, band], axis=1)], axis=0)

    def smooth(b, s):
        base = (b % 2) * (FB * cpitch)
        flats = []
        for u in range(2):
            parts = [cross_t[pl.ds(base + odd * cpitch + s + u + half * nsrc, FB // 2, stride=2 * cpitch)]
                     for odd in range(2) for half in range(2)]
            flats.append(jnp.concatenate(parts, axis=0).astype(jnp.bfloat16))
        total = lax.dot_general(bands, jnp.concatenate(flats, axis=1), (((1,), (1,)), ((), ())),
                                preferred_element_type=jnp.float32).astype(jnp.bfloat16)
        rows = pl.ds(pl.multiple_of(s * nchan, nchan), 2 * nchan)
        flat_ref[rows, pl.ds(pl.multiple_of(b * FB, FB), FB)] = total[:, 0:FB]
        flat_ref[rows, pl.ds(pl.multiple_of((nblk + b) * FB, FB), FB)] = total[:, FB:]

    load_first.wait()

    def prepare_first(k, carry):
        prepare(first, k)
        return carry

    lax.fori_loop(0, per, prepare_first, 0, unroll=True)

    @pl.when(me == 0)
    def _():
        halo[0] = jnp.zeros(halo.shape[1:], halo.dtype)
        halo_valid[0] = jnp.zeros(halo_valid.shape[1:], halo_valid.dtype)

    @pl.when(me == size - 1)
    def _():
        halo[1] = jnp.zeros(halo.shape[1:], halo.dtype)
        halo_valid[1] = jnp.zeros(halo_valid.shape[1:], halo_valid.dtype)

    def clear():
        def some(f, carry):
            cross_t[pl.ds(pl.multiple_of(f * 8 * cpitch, 8), 8 * cpitch)] = jnp.zeros((8 * cpitch, FB), jnp.float32)
            return carry

        lax.fori_loop(0, 2 * FB // 8, some, 0)
        for slot in range(nblk):
            for c in range(nchan + 2 * HALO, nrow):
                chan_t[pl.ds((slot * nrow + c) * pitch, pitch)] = jnp.zeros((pitch, depth), jnp.float32)

    def step(t, p):
        @pl.when(t == loaded)
        def _():
            for b in range(nblk):
                load(b).wait()

        @pl.when(t == loaded + 1)
        def _():
            clear()
            from_neighbours()

        for b in range(FIRST_EDGES, nblk):
            @pl.when(t == settled + per * (b + 1) - EARLY)
            def _():
                to_neighbours(lambda copy: copy.start(), [b])

        guarded(t, True, functools.partial(enter, t, p))
        for q in range(2):
            relay_in(q, t, p)
        for q in range(2):
            at = lag(rooted[q])
            odd = (p - at) % 2
            guarded(t - at, at_root[q][odd], functools.partial(reach_root, q, t - at, odd))
        now = t - settled

        @pl.when((now >= 0) & (now < per))
        def _():
            back(now, 1 - core).wait_recv()
            settle(now)

        @pl.when((now >= per) & (now < n))
        def _():
            back(now, 1 - core).wait_recv()
            b, lot = now // per - 1, now % per
            for u in range(0, nsrc // per, 2):
                smooth(jnp.maximum(b - 1, 0), lot * (nsrc // per) + u)
            for u in range(0, FB // per, 2):
                correlate(b, lot * (FB // per) + u)
            settle(now)

        for q in range(2):
            relay_on(q, t, p)
        for q in range(2):
            at = lag(summed[q])
            odd = (p - at) % 2
            guarded(t - at, at_root[q][odd], functools.partial(finish, q, t - at, odd))
        for q in range(2):
            spread(q, t, p)
        guarded(t - spread_at, True, lambda: back(t - spread_at, core).start())
        later = t + AHEAD
        guarded(later, later >= per, lambda: prepare(spec.at[later // per], later))
        guarded(t - turn_at, True, functools.partial(turn, t - turn_at))
        for b in range(nblk):
            @pl.when(t == settled + per * (b + 1) - 1)
            def _():
                turn_edges(b)


    def steps(tt, carry):
        for p in range(2):
            step(2 * tt + p, p)
        return carry

    total = n + settled
    lax.fori_loop(0, total // 2, steps, 0)
    if total % 2:
        step(jnp.int32(total - 1), (total - 1) % 2)

    for s in range(0, nsrc if nblk > 1 else 0, 2):
        smooth(nblk - 2, s)
    for f in range(0, FB, 2):
        correlate(nblk - 1, f)
    for s in range(0, nsrc, 2):
        smooth(nblk - 1, s)
    all_sent()
    to_neighbours(lambda copy: copy.wait_send())
    to_neighbours(lambda copy: copy.wait_send(), range(nblk))


def lag_kernel(scale, flat_ref, table_ref, out_ref, lags, sems):
    half = table_ref.shape[1]
    rows = lags.shape[1]
    copies = []
    for piece in range(PIECES):
        at = pl.ds(piece * rows, rows)
        even = jnp.dot(flat_ref[at, 0:half], table_ref[0:half], preferred_element_type=jnp.float32)
        odd = jnp.dot(flat_ref[at, half:], table_ref[half:], preferred_element_type=jnp.float32)
        lags[piece, :, 0:half] = (even + odd) * scale
        lags[piece, :, half:] = (even - odd) * scale
        copy = pltpu.make_async_copy(lags.at[piece], out_ref.at[at], sems.at[piece])
        copy.start()
        copies.append(copy)
    for copy in copies:
        copy.wait()


def local(size, spectra, valid, sources):
    nchan, _, nwin, nbins = spectra.shape
    nsrc = sources.shape[0]
    depth, nlags = 2 * nwin, 2 * nbins
    vmem = pl.BlockSpec(memory_space=pltpu.VMEM)

    chips = size // 2
    inner = 1
    while (2 * inner) ** 2 <= chips and chips % (2 * inner) == 0:
        inner *= 2
    outer = chips // inner
    nblk = nbins // FB
    many = MANY
    n = nblk * nsrc // (2 * many)
    nrow = -(-(nchan + 2 * HALO) // 8) * 8
    pitch, cpitch = FB + 1, 2 * nsrc + 1
    chunks = lambda *lead: pltpu.VMEM(lead + (n, 2, many, nwin, FB), jnp.bfloat16)
    flat = pl.pallas_call(
        functools.partial(cross_kernel, outer, inner, nrow),
        out_shape=pltpu.VMEM((nsrc * nchan, nlags), jnp.bfloat16),
        in_specs=[pl.BlockSpec(memory_space=pltpu.MemorySpace.HBM)] * 3,
        out_specs=vmem,
        scratch_shapes=[pltpu.SMEM((nsrc,), jnp.int32), pltpu.VMEM((nchan, nwin), jnp.int32),
                        pltpu.VMEM((nchan, 2, nwin, FB), jnp.bfloat16),
                        pltpu.VMEM((nblk, nchan, 2, nwin, FB), jnp.bfloat16),
                        pltpu.VMEM((2, nblk, HALO, 2, nwin, FB), jnp.bfloat16),
                        pltpu.VMEM((2, 8, nwin), jnp.int32),
                        pltpu.VMEM((nchan, depth), jnp.float32),
                        pltpu.VMEM((nsrc, nwin, FB), jnp.bfloat16),
                        chunks(), chunks(), chunks(), chunks(2), chunks(2), chunks(2),
                        pltpu.VMEM((n, 2, 2, many, nwin, FB), jnp.bfloat16),
                        pltpu.VMEM((nblk * nrow * pitch, depth), jnp.float32),
                        pltpu.VMEM((2 * 2 * nsrc * pitch, depth), jnp.float32),
                        pltpu.VMEM((2 * FB * cpitch, FB), jnp.float32),
                        pltpu.SemaphoreType.DMA((3 + nblk,)),
                        pltpu.SemaphoreType.DMA((2,)), pltpu.SemaphoreType.DMA((2, n)),
                        pltpu.SemaphoreType.DMA((6, 2, 2)), pltpu.SemaphoreType.DMA((6, 2, n)),
                        pltpu.SemaphoreType.DMA((2, nblk + 1)), pltpu.SemaphoreType.DMA((2, nblk + 1))],
        compiler_params=pltpu.CompilerParams(
            collective_id=0, has_side_effects=True, vmem_limit_bytes=56 << 20),
        name="cross",
    )(sources, valid, spectra)

    rows = nsrc * nchan // PIECES
    lags = pl.pallas_call(
        functools.partial(lag_kernel, 1.0 / (nwin * (2 * HALO + 1.0))),
        out_shape=jax.ShapeDtypeStruct((nsrc * nchan, nlags), jnp.float32),
        in_specs=[vmem, vmem],
        out_specs=pl.BlockSpec(memory_space=pltpu.MemorySpace.HBM),
        scratch_shapes=[pltpu.VMEM((PIECES, rows, nlags), jnp.float32), pltpu.SemaphoreType.DMA((PIECES,))],
        compiler_params=pltpu.CompilerParams(vmem_limit_bytes=24 << 20),
        name="lags",
    )(flat, jnp.asarray(make_table(nbins, nlags)))
    return lags.reshape(nsrc, nchan, nlags)


def solution(mesh):
    in_specs = (P(("grp", "chan"), None, None, None), P(("grp", "chan"), None), P("grp"))
    out_specs = P("grp", "chan", None)
    return jax.shard_map(functools.partial(local, mesh.shape["chan"]), mesh=mesh,
                         in_specs=in_specs, out_specs=out_specs, check_vma=False)
```
